256 devices in a mesh: seq: 128 (over z, y, x), head: 2 (over core).
Axes of the slice: x: 4, y: 4, z: 8, core: 2. Of those that a mesh axis runs over, the one named last changes fastest.
Arguments:
- queries: bfloat16 [65536, 2048], P(('seq', 'head')), may hold values from -6 to 6
- key_rows: bfloat16 [65536, 2048], P(('seq', 'head')), may hold values from -6 to 6
- values: bfloat16 [65536, 2048], P(('seq', 'head')), may hold values from -6 to 6
- out_grad: bfloat16 [65536, 2048], P(('seq', 'head')), may hold values from -6 to 6
- level_weights: float32 [16, 11], replicated, may hold values from 0.2 to 1
Outputs:
- query_grad: bfloat16 [65536, 2048], P(('seq', 'head'))
- key_grad: bfloat16 [65536, 2048], P(('seq', 'head'))
- value_grad: bfloat16 [65536, 2048], P(('seq', 'head'))
The draws below stay inside these ranges and needn't reach their ends.
All inputs are finite; a program needn't handle non-finite values.
Results may differ from the reference program's by a relative error of at most 0.003.
Values may be sent and summed in bfloat16 or wider, within the bound.
A program may use at most 128 MiB of HBM per device.

```python
import math
import jax
import jax.numpy as jnp
from jax import lax

HEADS = 16
DH = 128
D = 2048
BLOCK = 128
LEVELS = 11
TOKENS = 65536


def shard_levels(rng, dims, split, least, high):
    level = 1.0
    for dim, blocks in split:
        steps = jax.random.uniform(jax.random.fold_in(jax.random.fold_in(rng, 6), dim), (blocks,), jnp.float32, least / len(split), high / len(split))
        level = level * jnp.repeat(jnp.exp(steps), dims[dim] // blocks).reshape((-1,) + (1,) * (len(dims) - 1 - dim))
    return level


def centred(stream_key, shape, width, most, cuts=(), kind=jnp.bfloat16):
    array = width * jax.random.normal(stream_key, shape, jnp.float32)
    if cuts:
        array = array * shard_levels(stream_key, shape, cuts, -0.22, 0.18)
    return jnp.clip(array, -most, most).astype(kind)


def setup_inputs(seed: int = 0) -> dict:
    splits = jax.random.split(jax.random.key(seed), 6)
    queries = centred(splits[0], (TOKENS, D), 1.0, 6.0, ((0, 256),))
    key_rows = centred(splits[1], (TOKENS, D), 1.0, 6.0, ((0, 256),))
    values = centred(splits[2], (TOKENS, D), 1.0, 6.0, ((0, 256),))
    out_grad = centred(splits[3], (TOKENS, D), 1.0, 6.0, ((0, 256),))
    level_weights = jnp.clip(jnp.exp(jax.random.uniform(splits[4], (HEADS, LEVELS), jnp.float32, math.log(0.2), math.log(1.0))), 0.2, 1.0)
    return dict(queries=queries, key_rows=key_rows, values=values, out_grad=out_grad, level_weights=level_weights)


def fenwick_local(kv_blocks, qo_blocks, level_scale):
    block_count = kv_blocks.shape[0]
    inner_shape = kv_blocks.shape[1:]
    earlier = jnp.zeros_like(kv_blocks)
    later = jnp.zeros_like(qo_blocks)
    for level_index in range(1, block_count.bit_length()):
        half_span = 1 << level_index - 1
        group_count = block_count >> level_index
        weight = level_scale[:, level_index][:, None, None]
        kv_groups = kv_blocks.reshape((group_count, 2, half_span) + inner_shape)
        qo_groups = qo_blocks.reshape((group_count, 2, half_span) + inner_shape)
        lower_sum = lax.optimization_barrier(jnp.sum(kv_groups[:, 0], axis=1)) * weight
        upper_sum = lax.optimization_barrier(jnp.sum(qo_groups[:, 1], axis=1)) * weight
        zero_block = jnp.zeros_like(lower_sum)
        add_earlier = jnp.stack([zero_block, lower_sum], axis=1)[:, :, None]
        add_later = jnp.stack([upper_sum, zero_block], axis=1)[:, :, None]
        full_shape = (group_count, 2, half_span) + inner_shape
        earlier = earlier + jnp.broadcast_to(add_earlier, full_shape).reshape(kv_blocks.shape)
        later = later + jnp.broadcast_to(add_later, full_shape).reshape(qo_blocks.shape)
    return (earlier, later)

def block_grads(query_blk, key_blk, value_blk, grad_blk, level_scale):
    high = lax.Precision.HIGHEST
    block_len = query_blk.shape[1]
    query_f = query_blk.astype(jnp.float32)
    key_f = key_blk.astype(jnp.float32)
    value_f = value_blk.astype(jnp.float32)
    grad_f = grad_blk.astype(jnp.float32)
    rows = lax.broadcasted_iota(jnp.int32, (block_len, block_len), 0)
    cols = lax.broadcasted_iota(jnp.int32, (block_len, block_len), 1)
    causal_mask = (rows >= cols).astype(jnp.float32)
    first_weight = level_scale[:, 0][None, :, None, None]
    scores = jnp.einsum('nthd,nshd->nhts', query_f, key_f, precision=high)
    weighted = (scores * causal_mask * first_weight).astype(jnp.bfloat16)
    grad_prob = jnp.einsum('nthe,nshe->nhts', grad_f, value_f, precision=high)
    grad_score = (grad_prob * causal_mask * first_weight).astype(jnp.bfloat16)
    weighted_f = weighted.astype(jnp.float32)
    grad_score_f = grad_score.astype(jnp.float32)
    value_local = jnp.einsum('nhts,nthe->nshe', weighted_f, grad_f, precision=high)
    query_local = jnp.einsum('nhts,nshd->nthd', grad_score_f, key_f, precision=high)
    key_local = jnp.einsum('nhts,nthd->nshd', grad_score_f, query_f, precision=high)
    kv_blocks = jnp.einsum('nshd,nshe->nhde', key_f, value_f, precision=high)
    qo_blocks = jnp.einsum('nthd,nthe->nhde', query_f, grad_f, precision=high)
    earlier, later = fenwick_local(kv_blocks, qo_blocks, level_scale)
    query_cross = jnp.einsum('nthe,nhde->nthd', grad_f, earlier, precision=high)
    key_cross = jnp.einsum('nshe,nhde->nshd', value_f, later, precision=high)
    value_cross = jnp.einsum('nshd,nhde->nshe', key_f, later, precision=high)
    return ((query_local + query_cross).astype(jnp.bfloat16), (key_local + key_cross).astype(jnp.bfloat16), (value_local + value_cross).astype(jnp.bfloat16))

def reference(queries, key_rows, values, out_grad, level_weights):
    level_ids = jnp.arange(LEVELS, dtype=jnp.float32)
    level_scale = level_weights * jnp.exp2((1.0 - level_ids) / 2.0)[None, :] / jnp.sqrt(jnp.float32(DH * BLOCK))

    def per_head(packed):
        return packed.reshape(TOKENS // BLOCK, BLOCK, HEADS, DH).transpose(2, 0, 1, 3)[:, :, :, None, :]

    def one_head(items):
        query_blk, key_blk, value_blk, grad_blk, head_scale = items
        return block_grads(query_blk, key_blk, value_blk, grad_blk, head_scale)
    results = lax.map(one_head, (per_head(queries), per_head(key_rows), per_head(values), per_head(out_grad), level_scale[:, None, :]))

    def unpack(stacked):
        return stacked[:, :, :, 0, :].transpose(1, 2, 0, 3).reshape(TOKENS, HEADS * DH)
    return (unpack(results[0]), unpack(results[1]), unpack(results[2]))
```

```python
import functools

import jax
import jax.numpy as jnp
from jax import lax
from jax.experimental import pallas as pl
from jax.experimental.pallas import tpu as pltpu
from jax.sharding import PartitionSpec as P

DH = 128
BLOCK = 128
NX, NY, NZ = 4, 4, 8
PLANE = NX * NY
HEADS = 16
OWN = HEADS // 2
HALF = DH // 2
TOK = 256
MESH = pl.DeviceIdType.MESH
PRE = float(2.0**40)
POST = float(2.0**-40)
LEVEL_C = [float(2.0 ** ((1.0 - l) / 2.0) / 128.0) for l in range(11)]


def encode(x):
    s = x * PRE
    return (s * jnp.abs(s)).astype(jnp.bfloat16)


def decode(y):
    y = y.astype(jnp.float32)
    return y * (lax.rsqrt(jnp.maximum(jnp.abs(y), 1e-37)) * POST)


def dot_nn(a, b):
    return lax.dot_general(a, b, (((1,), (0,)), ((), ())), preferred_element_type=jnp.float32)


def dot_nt(a, b):
    return lax.dot_general(a, b, (((1,), (1,)), ((), ())), preferred_element_type=jnp.float32)


def dot_tn(a, b):
    return lax.dot_general(a, b, (((0,), (0,)), ((), ())), preferred_element_type=jnp.float32)


def split(x):
    hi = x.astype(jnp.bfloat16)
    lo = (x - hi.astype(jnp.float32)).astype(jnp.bfloat16)
    return hi, lo


def kernel(
    lw, q_hbm, k_hbm, v_hbm, o_hbm, qg_hbm, kg_hbm, vg_hbm,
    qs, ks, vs, os_, sums, kv0, qo1, from_core, from_core_x,
    send1, recv1, zsend, zrecv, send3, recv3, fwd3, plane_buf, part_q, part_k, part_v,
    out_q, out_k, out_v,
    in_sem, d_send, d_recv, x_send, x_recv, s1_send, s1_recv, z_send, z_recv,
    s3_send, s3_recv, f_send, f_recv, out_sem,
):
    seq = lax.axis_index("seq")
    core = lax.axis_index("head")
    x = lax.rem(seq, NX)
    y = lax.rem(lax.div(seq, NX), NY)
    z = lax.div(seq, PLANE)
    me = y * NX + x
    pair = lax.div(me, 2)
    sibling = (seq, 1 - core)

    def chip(i):
        return (z * PLANE + i, core)

    loads = []
    for n, (src, dst) in enumerate(((k_hbm, ks), (v_hbm, vs), (q_hbm, qs), (o_hbm, os_))):
        c = pltpu.make_async_copy(src, dst, in_sem.at[n])
        c.start()
        loads.append(c)

    barrier = pltpu.get_barrier_semaphore()
    pl.semaphore_signal(barrier, inc=1, device_id=sibling, device_id_type=MESH)
    for d in range(1, PLANE):
        pl.semaphore_signal(
            barrier, inc=1, device_id=chip(lax.rem(me + d, PLANE)), device_id_type=MESH
        )
    for d in range(1, NZ):
        pl.semaphore_signal(
            barrier,
            inc=1,
            device_id=(lax.rem(z + d, NZ) * PLANE + me, core),
            device_id_type=MESH,
        )
    pl.semaphore_wait(barrier, 1 + PLANE - 1 + NZ - 1)
    for c in loads:
        c.wait()

    def cols(h):
        return pl.ds(pl.multiple_of(h * DH, DH), DH)

    def states(h):
        c = cols(h)
        kv_a = dot_tn(vs[0:BLOCK, c], ks[0:BLOCK, c])
        kv_b = dot_tn(vs[BLOCK:TOK, c], ks[BLOCK:TOK, c])
        qo_a = dot_tn(qs[0:BLOCK, c], os_[0:BLOCK, c])
        qo_b = dot_tn(qs[BLOCK:TOK, c], os_[BLOCK:TOK, c])
        kv0[h] = kv_a
        qo1[h] = qo_b
        return kv_a + kv_b, qo_a + qo_b

    def to_core(j):
        return pltpu.make_async_remote_copy(
            src_ref=sums.at[(1 - core) * OWN + j],
            dst_ref=from_core.at[j],
            send_sem=d_send.at[j],
            recv_sem=d_recv.at[j],
            device_id=sibling,
            device_id_type=MESH,
        )

    def order(r):
        return lax.rem(pair + 1 + r, OWN)

    def first(r, _):
        j = order(r)
        h = (1 - core) * OWN + j
        kv, qo = states(h)
        sums[h, 0] = kv
        sums[h, 1] = qo
        to_core(j).start()
        return 0

    lax.fori_loop(0, OWN, first, 0)

    def plane_copy(i):
        return pltpu.make_async_remote_copy(
            src_ref=send1.at[i],
            dst_ref=recv1.at[me],
            send_sem=s1_send.at[i],
            recv_sem=s1_recv.at[me],
            device_id=chip(i),
            device_id_type=MESH,
        )

    def second(r, _):
        j = order(r)
        h = core * OWN + j
        kv, qo = states(h)
        sums[h, 0] = kv
        sums[h, 1] = qo
        to_core(j).wait_recv()
        for half in range(2):
            rows = slice(half * HALF, (half + 1) * HALF)
            i = 2 * j + half
            send1[i, 0] = encode(kv[rows] + from_core[j, 0, rows])
            send1[i, 1] = encode(qo[rows] + from_core[j, 1, rows])

            @pl.when(i != me)
            def _():
                plane_copy(i).start()

        return 0

    lax.fori_loop(0, OWN, second, 0)
    recv1[me] = send1[me]

    extra = pltpu.make_async_remote_copy(
        src_ref=sums.at[pl.ds(core * OWN, OWN), core],
        dst_ref=from_core_x,
        send_sem=x_send,
        recv_sem=x_recv,
        device_id=sibling,
        device_id_type=MESH,
    )
    extra.start()

    row = lax.broadcasted_iota(jnp.int32, (BLOCK, BLOCK), 0)
    col = lax.broadcasted_iota(jnp.int32, (BLOCK, BLOCK), 1)
    lower = row >= col
    upper = row <= col

    def local(h, _):
        c = cols(h)
        w0 = lw[h, 0] * LEVEL_C[0]
        w1 = lw[h, 1] * LEVEL_C[1]
        for b in range(2):
            rows = slice(b * BLOCK, (b + 1) * BLOCK)
            qb, kb, vb, ob = qs[rows, c], ks[rows, c], vs[rows, c], os_[rows, c]
            w_t = jnp.where(upper, dot_nt(kb, qb) * w0, 0.0).astype(jnp.bfloat16)
            g_t = jnp.where(upper, dot_nt(vb, ob) * w0, 0.0).astype(jnp.bfloat16)
            g = jnp.where(lower, dot_nt(ob, vb) * w0, 0.0).astype(jnp.bfloat16)
            ql = dot_nn(g, kb)
            kl = dot_nn(g_t, qb)
            vl = dot_nn(w_t, ob)
            if b == 1:
                hi, lo = split(kv0[h] * w1)
                ql = ql + (dot_nn(ob, hi) + dot_nn(ob, lo))
            else:
                hi, lo = split(qo1[h] * w1)
                kl = kl + (dot_nt(vb, hi) + dot_nt(vb, lo))
                vl = vl + (dot_nn(kb, hi) + dot_nn(kb, lo))
            part_q[rows, c] = ql
            part_k[rows, c] = kl
            part_v[rows, c] = vl
        return 0

    lax.fori_loop(0, HEADS, local, 0)

    hs = core * OWN + pair

    def weight(level):
        return lw[hs, level] * LEVEL_C[level]

    def plane_wait(i):
        return pltpu.make_async_remote_copy(
            src_ref=send1.at[i],
            dst_ref=recv1.at[i],
            send_sem=s1_send.at[i],
            recv_sem=s1_recv.at[i],
            device_id=chip(i),
            device_id_type=MESH,
        )

    def wait_plane(d, _):
        plane_wait(lax.rem(me + d, PLANE)).wait_recv()
        return 0

    lax.fori_loop(1, PLANE, wait_plane, 0)

    for kind in range(2):
        nodes = [decode(recv1[i, kind]) for i in range(PLANE)]
        tree = [nodes]
        while len(tree[-1]) > 1:
            last = tree[-1]
            tree.append([last[n] + last[n + 1] for n in range(0, len(last), 2)])
        zsend[kind] = encode(tree[-1][0])
        down = [None]
        for level in range(len(tree) - 2, -1, -1):
            w = weight(3 + level)
            new = []
            for n, parent in enumerate(down):
                a, b = tree[level][2 * n], tree[level][2 * n + 1]
                from_a, from_b = parent, parent
                if kind == 0:
                    from_b = a * w if parent is None else parent + a * w
                else:
                    from_a = b * w if parent is None else parent + b * w
                new += [from_a, from_b]
            down = new
        for i in range(PLANE):
            value = down[i]
            plane_buf[i, kind] = jnp.zeros((HALF, DH), jnp.float32) if value is None else value

    def z_copy(d):
        other = lax.rem(z + d, NZ)
        which = lax.select(other > z, 0, 1)
        return pltpu.make_async_remote_copy(
            src_ref=zsend.at[which],
            dst_ref=zrecv.at[d - 1],
            send_sem=z_send.at[d - 1],
            recv_sem=z_recv.at[d - 1],
            device_id=(other * PLANE + me, core),
            device_id_type=MESH,
        )

    z_copies = [z_copy(d) for d in range(1, NZ)]
    for c in z_copies:
        c.start()
    z_e = jnp.zeros((HALF, DH), jnp.float32)
    z_l = jnp.zeros((HALF, DH), jnp.float32)
    for d in range(1, NZ):
        z_copies[d - 1].wait_recv()
        src = lax.rem(z + NZ - d, NZ)
        diff = src ^ z
        w = lax.select(diff >= 4, weight(9), lax.select(diff >= 2, weight(8), weight(7)))
        value = decode(zrecv[d - 1]) * w
        z_e = z_e + lax.select(src < z, 1.0, 0.0) * value
        z_l = z_l + lax.select(src < z, 0.0, 1.0) * value

    def back_copy(i):
        return pltpu.make_async_remote_copy(
            src_ref=send3.at[i],
            dst_ref=recv3.at[me],
            send_sem=s3_send.at[i],
            recv_sem=s3_recv.at[me],
            device_id=chip(i),
            device_id_type=MESH,
        )

    for d in range(1, PLANE + 1):
        i = lax.rem(me + d, PLANE)
        send3[i, 0] = encode(plane_buf[i, 0] + z_e)
        send3[i, 1] = encode(plane_buf[i, 1] + z_l)
        if d < PLANE:
            back_copy(i).start()
        else:
            recv3[i] = send3[i]

    def back_wait(i):
        return pltpu.make_async_remote_copy(
            src_ref=send3.at[i],
            dst_ref=recv3.at[i],
            send_sem=s3_send.at[i],
            recv_sem=s3_recv.at[i],
            device_id=chip(i),
            device_id_type=MESH,
        )

    def forward(i):
        return pltpu.make_async_remote_copy(
            src_ref=recv3.at[i],
            dst_ref=fwd3.at[i],
            send_sem=f_send.at[i],
            recv_sem=f_recv.at[i],
            device_id=sibling,
            device_id_type=MESH,
        )

    extra.wait_recv()
    up = lax.select(core == 1, 1.0, 0.0)
    dn = 1.0 - up

    def stores(h):
        c = cols(h)
        return [
            pltpu.make_async_copy(s.at[:, c], t.at[:, c], out_sem.at[n, h])
            for n, (s, t) in enumerate(((out_q, qg_hbm), (out_k, kg_hbm), (out_v, vg_hbm)))
        ]

    def finish(h, cross_e, cross_l):
        c = cols(h)
        e_hi, e_lo = split(cross_e)
        l_hi, l_lo = split(cross_l)
        ob, vb, kb = os_[:, c], vs[:, c], ks[:, c]
        out_q[:, c] = (part_q[:, c] + (dot_nn(ob, e_hi) + dot_nn(ob, e_lo))).astype(jnp.bfloat16)
        out_k[:, c] = (part_k[:, c] + (dot_nt(vb, l_hi) + dot_nt(vb, l_lo))).astype(jnp.bfloat16)
        out_v[:, c] = (part_v[:, c] + (dot_nn(kb, l_hi) + dot_nn(kb, l_lo))).astype(jnp.bfloat16)
        for s in stores(h):
            s.start()

    def whole(buf, j, kind):
        return decode(jnp.concatenate([buf[2 * j, kind], buf[2 * j + 1, kind]], axis=0))

    def own_head(r, _):
        j = lax.rem(pair + r, OWN)
        for half in range(2):
            i = 2 * j + half

            @pl.when(i != me)
            def _():
                back_wait(i).wait_recv()

            forward(i).start()
        h = core * OWN + j
        w2 = lw[h, 2] * LEVEL_C[2]
        finish(
            h,
            whole(recv3, j, 0) + (w2 * up) * from_core[j, 0],
            whole(recv3, j, 1) + (w2 * dn) * from_core[j, 1],
        )
        return 0

    lax.fori_loop(0, OWN, own_head, 0)

    def other_head(r, _):
        j = lax.rem(pair + r, OWN)
        for half in range(2):
            forward(2 * j + half).wait_recv()
        h = (1 - core) * OWN + j
        w2 = lw[h, 2] * LEVEL_C[2]
        finish(
            h,
            whole(fwd3, j, 0) + (w2 * up) * from_core_x[j],
            whole(fwd3, j, 1) + (w2 * dn) * from_core_x[j],
        )
        return 0

    lax.fori_loop(0, OWN, other_head, 0)

    def drain_core(j, _):
        to_core(j).wait_send()
        return 0

    lax.fori_loop(0, OWN, drain_core, 0)
    extra.wait_send()
    for c in z_copies:
        c.wait_send()

    def drain_plane(d, _):
        i = lax.rem(me + d, PLANE)
        plane_copy(i).wait_send()
        back_copy(i).wait_send()
        return 0

    lax.fori_loop(1, PLANE, drain_plane, 0)

    def drain_forward(i, _):
        forward(i).wait_send()
        return 0

    lax.fori_loop(0, PLANE, drain_forward, 0)

    def drain_out(h, _):
        for s in stores(h):
            s.wait()
        return 0

    lax.fori_loop(0, HEADS, drain_out, 0)


def body(queries, key_rows, values, out_grad, level_weights):
    any_spec = pl.BlockSpec(memory_space=pl.ANY)
    bf, f32 = jnp.bfloat16, jnp.float32
    dma = pltpu.SemaphoreType.DMA
    rows = (TOK, HEADS * DH)
    out = jax.ShapeDtypeStruct(rows, bf)
    return tuple(
        pl.pallas_call(
            kernel,
            name="fenwick",
            out_shape=(out, out, out),
            in_specs=[pl.BlockSpec(memory_space=pltpu.SMEM)] + [any_spec] * 4,
            out_specs=(any_spec,) * 3,
            scratch_shapes=[pltpu.VMEM(rows, bf)] * 4
            + [
                pltpu.VMEM((HEADS, 2, DH, DH), f32),
                pltpu.VMEM((HEADS, DH, DH), f32),
                pltpu.VMEM((HEADS, DH, DH), f32),
                pltpu.VMEM((OWN, 2, DH, DH), f32),
                pltpu.VMEM((OWN, DH, DH), f32),
                pltpu.VMEM((PLANE, 2, HALF, DH), bf),
                pltpu.VMEM((PLANE, 2, HALF, DH), bf),
                pltpu.VMEM((2, HALF, DH), bf),
                pltpu.VMEM((NZ - 1, HALF, DH), bf),
                pltpu.VMEM((PLANE, 2, HALF, DH), bf),
                pltpu.VMEM((PLANE, 2, HALF, DH), bf),
                pltpu.VMEM((PLANE, 2, HALF, DH), bf),
                pltpu.VMEM((PLANE, 2, HALF, DH), f32),
            ]
            + [pltpu.VMEM(rows, f32)] * 3
            + [pltpu.VMEM(rows, bf)] * 3
            + [
                dma((4,)),
                dma((OWN,)),
                dma((OWN,)),
                dma,
                dma,
                dma((PLANE,)),
                dma((PLANE,)),
                dma((NZ - 1,)),
                dma((NZ - 1,)),
                dma((PLANE,)),
                dma((PLANE,)),
                dma((PLANE,)),
                dma((PLANE,)),
                dma((3, HEADS)),
            ],
            compiler_params=pltpu.CompilerParams(
                collective_id=0, has_side_effects=True, vmem_limit_bytes=48 << 20
            ),
        )(level_weights, queries, key_rows, values, out_grad)
    )


def solution(mesh):
    rows = P(("seq", "head"), None)
    return jax.shard_map(
        body,
        mesh=mesh,
        in_specs=(rows, rows, rows, rows, P()),
        out_specs=(rows, rows, rows),
        check_vma=False,
    )
```

```python
import functools

import jax
import jax.numpy as jnp
from jax import lax
from jax.experimental import pallas as pl
from jax.experimental.pallas import tpu as pltpu
from jax.sharding import PartitionSpec as P

DH = 128
BLOCK = 128
NX, NY, NZ = 4, 4, 8
PLANE = NX * NY
HEADS = 16
OWN = HEADS // 2
HALF = DH // 2
TOK = 256
MESH = pl.DeviceIdType.MESH
GROUP = 4
LOCAL_GROUP = 2
SPLIT_A = 4
LOAD_PARTS = 2
STORE_PARTS = 4
PRE = float(2.0**40)
POST = float(2.0**-40)
LEVEL_C = [float(2.0 ** ((1.0 - l) / 2.0) / 128.0) for l in range(11)]


def encode(x):
    s = x * PRE
    return (s * jnp.abs(s)).astype(jnp.bfloat16)


def decode(y):
    y = y.astype(jnp.float32)
    return y * (lax.rsqrt(jnp.maximum(jnp.abs(y), 1e-37)) * POST)


def dot_nn(a, b):
    return lax.dot_general(a, b, (((1,), (0,)), ((), ())), preferred_element_type=jnp.float32)


def dot_nt(a, b):
    return lax.dot_general(a, b, (((1,), (1,)), ((), ())), preferred_element_type=jnp.float32)


def dot_tn(a, b):
    return lax.dot_general(a, b, (((0,), (0,)), ((), ())), preferred_element_type=jnp.float32)


def split(x):
    hi = x.astype(jnp.bfloat16)
    lo = (x - hi.astype(jnp.float32)).astype(jnp.bfloat16)
    return hi, lo


def kernel(
    lw_hbm, q_hbm, k_hbm, v_hbm, o_hbm, out_q, out_k, out_v,
    lw, qs, ks, vs, os_, sums, to_sibling, to_extra, from_core, from_core_x,
    send1, recv1, zsend, zrecv, z_total, send3, recv3, fwd3, plane_buf, part_q, part_k, part_v,
    in_sem, d_send, d_recv, x_send, x_recv, z_ready, s1_send, s1_recv, z_send, z_recv,
    s3_send, s3_recv, f_send, f_recv,
):
    seq = lax.axis_index("seq")
    core = lax.axis_index("head")
    x = lax.rem(seq, NX)
    y = lax.rem(lax.div(seq, NX), NY)
    z = lax.div(seq, PLANE)
    me = y * NX + x
    pair = lax.div(me, 2)
    sibling = (seq, 1 - core)

    def chip(i):
        return (z * PLANE + i, core)

    width = OWN * DH
    loads = []
    stages = [(arrays, owner) for arrays in ("qo", "kv") for owner in (1 - core, core)]
    where = dict(q=(q_hbm, qs), k=(k_hbm, ks), v=(v_hbm, vs), o=(o_hbm, os_))
    for n, (arrays, owner) in enumerate(stages):
        half = pl.ds(pl.multiple_of(owner * width, width), width)
        loads.append([])
        for array in arrays:
            src, dst = where[array]
            for p in range(LOAD_PARTS):
                rows = pl.ds(p * (TOK // LOAD_PARTS), TOK // LOAD_PARTS)
                loads[n].append(
                    pltpu.make_async_copy(src.at[rows, half], dst.at[rows, half], in_sem.at[n])
                )
    loads.append([pltpu.make_async_copy(lw_hbm, lw, in_sem.at[4])])

    def start_loads(lo, hi):
        for stage in loads[lo:hi]:
            for c in stage:
                c.start()

    def wait_loads(n):
        if n < 4:
            drain(qs, in_sem.at[n])
        else:
            loads[n][0].wait()

    start_loads(0, 2)
    barrier = pltpu.get_barrier_semaphore()
    pl.semaphore_signal(barrier, inc=1, device_id=sibling, device_id_type=MESH)
    for d in range(1, PLANE):
        pl.semaphore_signal(
            barrier, inc=1, device_id=chip(lax.rem(me + d, PLANE)), device_id_type=MESH
        )
    for d in range(1, NZ):
        other = lax.rem(z + d, NZ)

        @pl.when(other > z)
        def _():
            pl.semaphore_signal(
                barrier, inc=1, device_id=(other * PLANE + me, core), device_id_type=MESH
            )

    def wait_barrier():
        pl.semaphore_wait(barrier, PLANE + z)
        for d in range(1, NZ):
            other = lax.rem(z + d, NZ)

            @pl.when(other < z)
            def _():
                pl.semaphore_signal(
                    z_ready, inc=1, device_id=(other * PLANE + me, core), device_id_type=MESH
                )

    start_loads(2, 5)

    def drain(buf, sem):
        pltpu.make_async_copy(buf, buf, sem).wait()

    def cols(h):
        return pl.ds(pl.multiple_of(h * DH, DH), DH)

    def states(kind, h):
        a, b = (vs, ks) if kind == 0 else (qs, os_)
        c = cols(h)
        return dot_tn(a[:, c], b[:, c])

    def part(j):
        return lax.div(lax.rem(j - pair - 1 + 2 * OWN, OWN), GROUP)

    def to_core(kind, j):
        return pltpu.make_async_remote_copy(
            src_ref=to_sibling.at[kind, j],
            dst_ref=from_core.at[kind, j],
            send_sem=d_send.at[kind],
            recv_sem=d_recv.at[kind, part(j)],
            device_id=sibling,
            device_id_type=MESH,
        )

    def order(r):
        return lax.rem(pair + 1 + r, OWN)

    def group(g):
        return [order(g * GROUP + n) for n in range(GROUP)]

    def states_for_sibling(kind, g):
        values = [states(kind, (1 - core) * OWN + j) for j in group(g)]
        for j, value in zip(group(g), values):
            to_sibling[kind, j] = encode(value)

    def send_core(kind, g):
        for j in group(g):
            to_core(kind, j).start()

    def states_own(kind, g):
        values = [states(kind, core * OWN + j) for j in group(g)]
        for j, value in zip(group(g), values):
            sums[kind, j] = value

    def plane_copy(kind, i):
        return pltpu.make_async_remote_copy(
            src_ref=send1.at[kind, i],
            dst_ref=recv1.at[kind, me],
            send_sem=s1_send.at[kind],
            recv_sem=s1_recv.at[kind],
            device_id=chip(i),
            device_id_type=MESH,
        )

    def send_plane(kind, g):
        drain(from_core.at[kind, pl.ds(0, GROUP)], d_recv.at[kind, g])
        for j in group(g):
            for half in range(2):
                rows = pl.ds(half * HALF, HALF)
                total = sums[kind, j, rows] + decode(from_core[kind, j, rows])
                send1[kind, 2 * j + half] = encode(total)
        for j in group(g):
            for half in range(2):
                i = 2 * j + half

                @pl.when(i != me)
                def _():
                    plane_copy(kind, i).start()

    def keep_plane(kind):
        recv1[kind, me] = send1[kind, me]

    wait_loads(0)
    states_for_sibling(1, 0)
    wait_barrier()
    send_core(1, 0)
    states_for_sibling(1, 1)
    send_core(1, 1)
    wait_loads(1)
    states_own(1, 0)
    states_own(1, 1)
    send_plane(1, 0)
    send_plane(1, 1)
    keep_plane(1)
    wait_loads(2)
    states_for_sibling(0, 0)
    send_core(0, 0)
    states_for_sibling(0, 1)
    send_core(0, 1)
    wait_loads(3)
    states_own(0, 0)
    states_own(0, 1)
    wait_loads(4)

    row = lax.broadcasted_iota(jnp.int32, (BLOCK, BLOCK), 0)
    col = lax.broadcasted_iota(jnp.int32, (BLOCK, BLOCK), 1)
    lower = row >= col
    upper = row <= col

    A, B = slice(0, BLOCK), slice(BLOCK, TOK)

    def local_heads(first_head):
        heads = [first_head + n for n in range(LOCAL_GROUP)]
        data = []
        for h in heads:
            c = cols(h)
            data.append((qs[:, c], ks[:, c], vs[:, c], os_[:, c]))
        scores = []
        for qb, kb, vb, ob in data:
            scores.append(
                (
                    dot_nt(ob[A], vb[A]), dot_nt(ob[B], vb),
                    dot_nt(vb[A], ob), dot_nt(vb[B], ob[B]),
                    dot_nt(kb[A], qb), dot_nt(kb[B], qb[B]),
                )
            )
        weighted = []
        for h, (g_a, g_b, gt_a, gt_b, wt_a, wt_b) in zip(heads, scores):
            w0 = lw[h, 0] * LEVEL_C[0]
            w1 = lw[h, 1] * LEVEL_C[1]

            def masked(score, mask):
                return jnp.where(mask, score * w0, 0.0).astype(jnp.bfloat16)

            def level1(score):
                return (score * w1).astype(jnp.bfloat16)

            def join(a, b):
                return jnp.concatenate([a, b], axis=1)

            weighted.append(
                (
                    masked(g_a, lower), join(level1(g_b[:, A]), masked(g_b[:, B], lower)),
                    join(masked(gt_a[:, A], upper), level1(gt_a[:, B])), masked(gt_b, upper),
                    join(masked(wt_a[:, A], upper), level1(wt_a[:, B])), masked(wt_b, upper),
                )
            )
        results = []
        for (qb, kb, vb, ob), (g_a, g_b, gt_a, gt_b, wt_a, wt_b) in zip(data, weighted):
            results.append(
                (
                    dot_nn(g_a, kb[A]), dot_nn(g_b, kb),
                    dot_nn(gt_a, qb), dot_nn(gt_b, qb[B]),
                    dot_nn(wt_a, ob), dot_nn(wt_b, ob[B]),
                )
            )
        for h, values in zip(heads, results):
            c = cols(h)
            for n, part in enumerate((part_q, part_k, part_v)):
                part[A, c] = values[2 * n]
                part[B, c] = values[2 * n + 1]

    def local(lo, hi):
        def step(n, _):
            local_heads(lo + n * LOCAL_GROUP)
            return 0

        lax.fori_loop(0, (hi - lo) // LOCAL_GROUP, step, 0)

    extra = pltpu.make_async_remote_copy(
        src_ref=to_extra,
        dst_ref=from_core_x,
        send_sem=x_send,
        recv_sem=x_recv,
        device_id=sibling,
        device_id_type=MESH,
    )

    hs = core * OWN + pair

    def weight(level):
        return lw[hs, level] * LEVEL_C[level]

    def combine(kind):
        others = pl.ds(0, PLANE - 1)
        pltpu.make_async_copy(
            recv1.at[kind, others], recv1.at[kind, others], s1_recv.at[kind]
        ).wait()
        nodes = [decode(recv1[kind, i]) for i in range(PLANE)]
        tree = [nodes]
        while len(tree[-1]) > 1:
            last = tree[-1]
            tree.append([last[n] + last[n + 1] for n in range(0, len(last), 2)])
        zsend[kind] = encode(tree[-1][0])
        if kind == 0:

            @pl.when(z < NZ - 1)
            def _():
                pl.semaphore_wait(z_ready, NZ - 1 - z)

        for d in range(1, NZ):

            @pl.when(z_sends(kind, d))
            def _():
                z_copy(kind, d).start()

        down = [None]
        for level in range(len(tree) - 2, -1, -1):
            w = weight(3 + level)
            new = []
            for n, parent in enumerate(down):
                a, b = tree[level][2 * n], tree[level][2 * n + 1]
                from_a, from_b = parent, parent
                if kind == 0:
                    from_b = a * w if parent is None else parent + a * w
                else:
                    from_a = b * w if parent is None else parent + b * w
                new += [from_a, from_b]
            down = new
        for i in range(PLANE):
            value = down[i]
            plane_buf[kind, i] = jnp.zeros((HALF, DH), jnp.float32) if value is None else value

    def z_sends(kind, d):
        other = lax.rem(z + d, NZ)
        return other > z if kind == 0 else other < z

    def z_takes(kind, d):
        src = lax.rem(z + NZ - d, NZ)
        return src < z if kind == 0 else src > z

    def z_copy(kind, d):
        return pltpu.make_async_remote_copy(
            src_ref=zsend.at[kind],
            dst_ref=zrecv.at[d - 1],
            send_sem=z_send,
            recv_sem=z_recv.at[d - 1],
            device_id=(lax.rem(z + d, NZ) * PLANE + me, core),
            device_id_type=MESH,
        )

    def back_part(chip_pair, from_pair):
        return lax.div(lax.rem(from_pair - chip_pair + OWN, OWN), GROUP)

    def back_copy(kind, i):
        return pltpu.make_async_remote_copy(
            src_ref=send3.at[kind, i],
            dst_ref=recv3.at[kind, me],
            send_sem=s3_send.at[kind],
            recv_sem=s3_recv.at[kind, back_part(lax.div(i, 2), pair)],
            device_id=chip(i),
            device_id_type=MESH,
        )

    def give_back(kind):
        for d in range(1, NZ):

            @pl.when(z_takes(kind, d))
            def _():
                z_copy(kind, d).wait_recv()

        z_total[...] = jnp.zeros((HALF, DH), jnp.float32)
        for d in range(1, NZ):

            @pl.when(z_takes(kind, d))
            def _():
                diff = lax.rem(z + NZ - d, NZ) ^ z
                w = lax.select(diff >= 4, weight(9), lax.select(diff >= 2, weight(8), weight(7)))
                z_total[...] = z_total[...] + decode(zrecv[d - 1]) * w

        total = z_total[...]

        def step(d, _):
            i = lax.rem(me + d, PLANE)
            send3[kind, i] = encode(plane_buf[kind, i] + total)
            back_copy(kind, i).start()
            return 0

        lax.fori_loop(1, PLANE, step, 0, unroll=3)
        recv3[kind, me] = encode(plane_buf[kind, me] + total)

    def start_extra():
        def step(j, _):
            to_extra[j] = encode(sums[core, j])
            return 0

        lax.fori_loop(0, OWN, step, 0)
        extra.start()

    low = z < NZ // 2
    high = z >= NZ // 2

    def in_order(step):
        @pl.when(low)
        def _():
            step(0)
            step(1)

        @pl.when(high)
        def _():
            step(1)
            step(0)

    local(0, SPLIT_A)
    send_plane(0, 0)
    send_plane(0, 1)
    keep_plane(0)
    start_extra()
    local(SPLIT_A, HEADS)
    combine(1)
    combine(0)
    in_order(give_back)

    def forward(kind, j):
        slots = pl.ds(2 * j, 2)
        return pltpu.make_async_remote_copy(
            src_ref=recv3.at[kind, slots],
            dst_ref=fwd3.at[kind, slots],
            send_sem=f_send.at[kind],
            recv_sem=f_recv.at[kind, back_part(pair, j)],
            device_id=sibling,
            device_id_type=MESH,
        )

    def drain_early():
        extra.wait_send()
        drain(zrecv, z_send)
        for kind in range(2):
            drain(to_sibling.at[kind], d_send.at[kind])
            drain(send1.at[kind, pl.ds(0, PLANE - 1)], s1_send.at[kind])

    drain_early()
    extra.wait_recv()
    up = lax.select(core == 1, 1.0, 0.0)
    dn = 1.0 - up

    def finish(kind, heads, crosses):
        values = []
        for h, cross in zip(heads, crosses):
            c = cols(h)
            hi, lo = split(cross)
            stack = jnp.concatenate([hi, lo], axis=0)
            if kind == 0:
                ob = os_[:, c]
                more = dot_nn(jnp.concatenate([ob, ob], axis=1), stack)
                values.append((out_q, c, part_q[:, c] + more))
            else:
                vb, kb = vs[:, c], ks[:, c]
                wide = jnp.concatenate([hi, lo], axis=1)
                more = dot_nt(jnp.concatenate([vb, vb], axis=1), wide)
                values.append((out_k, c, part_k[:, c] + more))
                more = dot_nn(jnp.concatenate([kb, kb], axis=1), stack)
                values.append((out_v, c, part_v[:, c] + more))
        for ref, c, value in values:
            ref[:, c] = value.astype(jnp.bfloat16)

    def whole(buf, kind, j):
        return decode(jnp.concatenate([buf[kind, 2 * j], buf[kind, 2 * j + 1]], axis=0))

    def level2(kind, h):
        return lw[h, 2] * LEVEL_C[2] * (up if kind == 0 else dn)

    def back_group(g):
        return [lax.rem(pair + g * GROUP + n, OWN) for n in range(GROUP)]

    def pass_on(kind):
        for g in range(OWN // GROUP):
            slots = 2 * GROUP - (1 if g == 0 else 0)
            drain(recv3.at[kind, pl.ds(0, slots)], s3_recv.at[kind, g])
            for j in back_group(g):
                forward(kind, j).start()

    def own_heads(kind):
        def step(g, _):
            slots = back_group(g)
            heads = [core * OWN + j for j in slots]
            finish(
                kind,
                heads,
                [
                    whole(recv3, kind, j) + level2(kind, h) * decode(from_core[kind, j])
                    for j, h in zip(slots, heads)
                ],
            )
            return 0

        lax.fori_loop(0, OWN // GROUP, step, 0)

    def other_heads(kind):
        for g in range(OWN // GROUP):
            slots = back_group(g)
            drain(fwd3.at[kind, pl.ds(0, 2 * GROUP)], f_recv.at[kind, g])
            heads = [(1 - core) * OWN + j for j in slots]
            finish(
                kind,
                heads,
                [
                    whole(fwd3, kind, j) + level2(kind, h) * decode(from_core_x[j])
                    for j, h in zip(slots, heads)
                ],
            )

    def drain_late():
        for kind in range(2):
            drain(send3.at[kind, pl.ds(0, PLANE - 1)], s3_send.at[kind])
            drain(fwd3.at[kind], f_send.at[kind])

    def finish_all(kind):
        pass_on(kind)
        own_heads(kind)
        other_heads(kind)

    in_order(finish_all)
    drain_late()


def store(a, b, c, x, y, z, sem):
    part = TOK // STORE_PARTS
    copies = []
    for n, (src, dst) in enumerate(((a, x), (b, y), (c, z))):
        for p in range(STORE_PARTS):
            rows = pl.ds(p * part, part)
            copies.append(pltpu.make_async_copy(src.at[rows], dst.at[rows], sem.at[n, p]))
    for copy in copies:
        copy.start()
    for copy in copies:
        copy.wait()


def body(queries, key_rows, values, out_grad, level_weights):
    any_spec = pl.BlockSpec(memory_space=pl.ANY)
    hbm = pl.BlockSpec(memory_space=pltpu.HBM)
    vmem = pl.BlockSpec(memory_space=pltpu.VMEM)
    bf, f32 = jnp.bfloat16, jnp.float32
    dma = pltpu.SemaphoreType.DMA
    rows = (TOK, HEADS * DH)
    out = jax.ShapeDtypeStruct(rows, bf)
    pinned = [
        pltpu.with_memory_space_constraint(a, pltpu.HBM)
        for a in (level_weights, queries, key_rows, values, out_grad)
    ]
    grads = pl.pallas_call(
        kernel,
        name="fenwick",
        out_shape=(pltpu.VMEM(rows, bf),) * 3,
        in_specs=[hbm] * 5,
        out_specs=(vmem,) * 3,
        scratch_shapes=[pltpu.SMEM((HEADS, 11), f32)]
        + [pltpu.VMEM(rows, bf)] * 4
        + [
            pltpu.VMEM((2, OWN, DH, DH), f32),
            pltpu.VMEM((2, OWN, DH, DH), bf),
            pltpu.VMEM((OWN, DH, DH), bf),
            pltpu.VMEM((2, OWN, DH, DH), bf),
            pltpu.VMEM((OWN, DH, DH), bf),
            pltpu.VMEM((2, PLANE, HALF, DH), bf),
            pltpu.VMEM((2, PLANE, HALF, DH), bf),
            pltpu.VMEM((2, HALF, DH), bf),
            pltpu.VMEM((NZ - 1, HALF, DH), bf),
            pltpu.VMEM((HALF, DH), f32),
            pltpu.VMEM((2, PLANE, HALF, DH), bf),
            pltpu.VMEM((2, PLANE, HALF, DH), bf),
            pltpu.VMEM((2, PLANE, HALF, DH), bf),
            pltpu.VMEM((2, PLANE, HALF, DH), f32),
        ]
        + [pltpu.VMEM(rows, f32)] * 3
        + [
            dma((5,)),
            dma((2,)),
            dma((2, OWN // GROUP)),
            dma,
            dma,
            pltpu.SemaphoreType.REGULAR,
            dma((2,)),
            dma((2,)),
            dma,
            dma((NZ - 1,)),
            dma((2,)),
            dma((2, OWN // GROUP)),
            dma((2,)),
            dma((2, OWN // GROUP)),
        ],
        compiler_params=pltpu.CompilerParams(
            collective_id=0, has_side_effects=True, vmem_limit_bytes=40 << 20
        ),
    )(*pinned)
    return tuple(
        pl.pallas_call(
            store,
            name="store",
            out_shape=(out, out, out),
            in_specs=[any_spec] * 3,
            out_specs=(hbm,) * 3,
            scratch_shapes=[dma((3, STORE_PARTS))],
        )(*(pltpu.with_memory_space_constraint(g, pltpu.VMEM) for g in grads))
    )


def solution(mesh):
    rows = P(("seq", "head"), None)
    return jax.shard_map(
        body,
        mesh=mesh,
        in_specs=(rows, rows, rows, rows, P()),
        out_specs=(rows, rows, rows),
        check_vma=False,
    )
```

```python
import functools

import jax
import jax.numpy as jnp
from jax import lax
from jax.experimental import pallas as pl
from jax.experimental.pallas import tpu as pltpu
from jax.sharding import PartitionSpec as P

DH = 128
BLOCK = 128
NX, NY, NZ = 4, 4, 8
PLANE = NX * NY
BACK_ORDER = sorted(
    range(PLANE), key=lambda i: (min(i % NX, NX - i % NX) + min(i // NX, NY - i // NX), i)
)
HEADS = 16
OWN = HEADS // 2
HALF = DH // 2
TOK = 256
MESH = pl.DeviceIdType.MESH
GROUP = 4
LOCAL_GROUP = 2
SPLIT_A, SPLIT_B = 10, 10
LOAD_PARTS = 2
STORE_PARTS = 4
PRE = float(2.0**40)
POST = float(2.0**-40)
LEVEL_C = [float(2.0 ** ((1.0 - l) / 2.0) / 128.0) for l in range(11)]


def encode(x):
    s = x * PRE
    return (s * jnp.abs(s)).astype(jnp.bfloat16)


def decode(y):
    y = y.astype(jnp.float32)
    return y * (lax.rsqrt(jnp.maximum(jnp.abs(y), 1e-37)) * POST)


def dot_nn(a, b):
    return lax.dot_general(a, b, (((1,), (0,)), ((), ())), preferred_element_type=jnp.float32)


def dot_nt(a, b):
    return lax.dot_general(a, b, (((1,), (1,)), ((), ())), preferred_element_type=jnp.float32)


def dot_tn(a, b):
    return lax.dot_general(a, b, (((0,), (0,)), ((), ())), preferred_element_type=jnp.float32)


def split(x):
    hi = x.astype(jnp.bfloat16)
    lo = (x - hi.astype(jnp.float32)).astype(jnp.bfloat16)
    return hi, lo


def kernel(
    lw_hbm, q_hbm, k_hbm, v_hbm, o_hbm,
    out_q, out_k, out_v, fwd3, base_x, part_k, part_v, ks, vs,
    lw, qs, os_, sums, to_sibling, to_extra, from_core, from_core_x,
    send1, recv1, zsend, zrecv, z_total, send3, recv3, plane_buf, part_q,
    in_sem, d_send, d_recv, x_send, x_recv, z_ready, s1_send, s1_recv, z_send, z_recv,
    s3_send, s3_recv, f_send, f_recv,
):
    seq = lax.axis_index("seq")
    core = lax.axis_index("head")
    x = lax.rem(seq, NX)
    y = lax.rem(lax.div(seq, NX), NY)
    z = lax.div(seq, PLANE)
    me = y * NX + x
    pair = lax.div(me, 2)
    sibling = (seq, 1 - core)

    def chip(i):
        return (z * PLANE + i, core)

    width = OWN * DH
    loads = []
    stages = [(arrays, owner) for arrays in ("qo", "kv") for owner in (1 - core, core)]
    where = dict(q=(q_hbm, qs), k=(k_hbm, ks), v=(v_hbm, vs), o=(o_hbm, os_))
    for n, (arrays, owner) in enumerate(stages):
        half = pl.ds(pl.multiple_of(owner * width, width), width)
        loads.append([])
        for array in arrays:
            src, dst = where[array]
            for p in range(LOAD_PARTS):
                rows = pl.ds(p * (TOK // LOAD_PARTS), TOK // LOAD_PARTS)
                loads[n].append(
                    pltpu.make_async_copy(src.at[rows, half], dst.at[rows, half], in_sem.at[n])
                )
    loads.append([pltpu.make_async_copy(lw_hbm, lw, in_sem.at[4])])

    def start_loads(lo, hi):
        for stage in loads[lo:hi]:
            for c in stage:
                c.start()

    def wait_loads(n):
        if n < 4:
            drain(qs, in_sem.at[n])
        else:
            loads[n][0].wait()

    barrier = pltpu.get_barrier_semaphore()
    pl.semaphore_signal(barrier, inc=1, device_id=sibling, device_id_type=MESH)
    for d in (10, 6, 9, 11, 14, 2, 8, 5, 7, 13, 15, 1, 3, 4, 12):
        pl.semaphore_signal(
            barrier, inc=1, device_id=chip(lax.rem(me + d, PLANE)), device_id_type=MESH
        )
    for d in range(1, NZ):
        other = lax.rem(z + d, NZ)

        @pl.when(other > z)
        def _():
            pl.semaphore_signal(
                barrier, inc=1, device_id=(other * PLANE + me, core), device_id_type=MESH
            )

    start_loads(0, 2)

    def wait_barrier():
        pl.semaphore_wait(barrier, PLANE + z)
        for d in range(1, NZ):
            other = lax.rem(z + d, NZ)

            @pl.when(other < z)
            def _():
                pl.semaphore_signal(
                    z_ready, inc=1, device_id=(other * PLANE + me, core), device_id_type=MESH
                )

    def drain(buf, sem):
        pltpu.make_async_copy(buf, buf, sem).wait()

    def cols(h):
        return pl.ds(pl.multiple_of(h * DH, DH), DH)

    def states(kind, h):
        a, b = (vs, ks) if kind == 0 else (qs, os_)
        c = cols(h)
        return dot_tn(a[:, c], b[:, c])

    def part(j):
        return lax.div(lax.rem(j - pair - 1 + 2 * OWN, OWN), GROUP)

    def to_core(kind, j):
        return pltpu.make_async_remote_copy(
            src_ref=to_sibling.at[kind, j],
            dst_ref=from_core.at[kind, j],
            send_sem=d_send.at[kind],
            recv_sem=d_recv.at[kind, part(j)],
            device_id=sibling,
            device_id_type=MESH,
        )

    def order(r):
        return lax.rem(pair + 1 + r, OWN)

    def group(g):
        return [order(g * GROUP + n) for n in range(GROUP)]

    def states_for_sibling(kind, g):
        values = [states(kind, (1 - core) * OWN + j) for j in group(g)]
        for j, value in zip(group(g), values):
            to_sibling[kind, j] = encode(value)

    def send_core(kind, g):
        for j in group(g):
            to_core(kind, j).start()

    def states_own(kind, g):
        values = [states(kind, core * OWN + j) for j in group(g)]
        for j, value in zip(group(g), values):
            sums[kind, j] = value

    def plane_copy(kind, i):
        return pltpu.make_async_remote_copy(
            src_ref=send1.at[kind, i],
            dst_ref=recv1.at[kind, me],
            send_sem=s1_send.at[kind],
            recv_sem=s1_recv.at[kind],
            device_id=chip(i),
            device_id_type=MESH,
        )

    def send_plane(kind, g):
        drain(from_core.at[kind, pl.ds(0, GROUP)], d_recv.at[kind, g])
        for j in group(g):
            for half in range(2):
                rows = pl.ds(half * HALF, HALF)
                total = sums[kind, j, rows] + decode(from_core[kind, j, rows])
                send1[kind, 2 * j + half] = encode(total)
        for j in group(g):
            for half in range(2):
                i = 2 * j + half

                @pl.when(i != me)
                def _():
                    plane_copy(kind, i).start()

    def keep_plane(kind):
        recv1[kind, me] = send1[kind, me]

    wait_loads(0)
    start_loads(2, 5)
    states_for_sibling(1, 0)
    states_for_sibling(1, 1)
    wait_loads(1)
    states_own(1, 0)
    wait_barrier()
    send_core(1, 0)
    send_core(1, 1)
    states_own(1, 1)
    send_plane(1, 0)
    send_plane(1, 1)
    keep_plane(1)
    wait_loads(2)
    states_for_sibling(0, 0)
    send_core(0, 0)
    states_for_sibling(0, 1)
    send_core(0, 1)
    wait_loads(3)
    states_own(0, 0)
    states_own(0, 1)
    wait_loads(4)

    row = lax.broadcasted_iota(jnp.int32, (BLOCK, BLOCK), 0)
    col = lax.broadcasted_iota(jnp.int32, (BLOCK, BLOCK), 1)
    lower = row >= col
    upper = row <= col

    A, B = slice(0, BLOCK), slice(BLOCK, TOK)

    def local_heads(first_head):
        heads = [first_head + n for n in range(LOCAL_GROUP)]
        data = []
        for h in heads:
            c = cols(h)
            data.append((qs[:, c], ks[:, c], vs[:, c], os_[:, c]))
        scores = []
        for qb, kb, vb, ob in data:
            scores.append(
                (
                    dot_nt(ob[A], vb[A]), dot_nt(ob[B], vb),
                    dot_nt(vb[A], ob), dot_nt(vb[B], ob[B]),
                    dot_nt(kb[A], qb), dot_nt(kb[B], qb[B]),
                )
            )
        weighted = []
        for h, (g_a, g_b, gt_a, gt_b, wt_a, wt_b) in zip(heads, scores):
            w0 = lw[h, 0] * LEVEL_C[0]
            w1 = lw[h, 1] * LEVEL_C[1]

            def masked(score, mask):
                return jnp.where(mask, score * w0, 0.0).astype(jnp.bfloat16)

            def level1(score):
                return (score * w1).astype(jnp.bfloat16)

            def join(a, b):
                return jnp.concatenate([a, b], axis=1)

            weighted.append(
                (
                    masked(g_a, lower), join(level1(g_b[:, A]), masked(g_b[:, B], lower)),
                    join(masked(gt_a[:, A], upper), level1(gt_a[:, B])), masked(gt_b, upper),
                    join(masked(wt_a[:, A], upper), level1(wt_a[:, B])), masked(wt_b, upper),
                )
            )
        results = []
        for (qb, kb, vb, ob), (g_a, g_b, gt_a, gt_b, wt_a, wt_b) in zip(data, weighted):
            results.append(
                (
                    dot_nn(g_a, kb[A]), dot_nn(g_b, kb),
                    dot_nn(gt_a, qb), dot_nn(gt_b, qb[B]),
                    dot_nn(wt_a, ob), dot_nn(wt_b, ob[B]),
                )
            )
        for h, values in zip(heads, results):
            c = cols(h)
            for n, part in enumerate((part_q, part_k, part_v)):
                part[A, c] = values[2 * n]
                part[B, c] = values[2 * n + 1]

    def local(lo, hi):
        def step(n, _):
            local_heads(lo + n * LOCAL_GROUP)
            return 0

        lax.fori_loop(0, (hi - lo) // LOCAL_GROUP, step, 0)

    extra = pltpu.make_async_remote_copy(
        src_ref=to_extra,
        dst_ref=from_core_x,
        send_sem=x_send,
        recv_sem=x_recv,
        device_id=sibling,
        device_id_type=MESH,
    )

    hs = core * OWN + pair

    def weight(level):
        return lw[hs, level] * LEVEL_C[level]

    def combine(kind):
        others = pl.ds(0, PLANE - 1)
        pltpu.make_async_copy(
            recv1.at[kind, others], recv1.at[kind, others], s1_recv.at[kind]
        ).wait()
        nodes = [decode(recv1[kind, i]) for i in range(PLANE)]
        tree = [nodes]
        while len(tree[-1]) > 1:
            last = tree[-1]
            tree.append([last[n] + last[n + 1] for n in range(0, len(last), 2)])
        zsend[kind] = encode(tree[-1][0])
        if kind == 0:

            @pl.when(z < NZ - 1)
            def _():
                pl.semaphore_wait(z_ready, NZ - 1 - z)

        for d in range(1, NZ):

            @pl.when(z_sends(kind, d))
            def _():
                z_copy(kind, d).start()

        down = [None]
        for level in range(len(tree) - 2, -1, -1):
            w = weight(3 + level)
            new = []
            for n, parent in enumerate(down):
                a, b = tree[level][2 * n], tree[level][2 * n + 1]
                from_a, from_b = parent, parent
                if kind == 0:
                    from_b = a * w if parent is None else parent + a * w
                else:
                    from_a = b * w if parent is None else parent + b * w
                new += [from_a, from_b]
            down = new
        for i in range(PLANE):
            value = down[i]
            plane_buf[kind, i] = jnp.zeros((HALF, DH), jnp.float32) if value is None else value

    def z_sends(kind, d):
        other = lax.rem(z + d, NZ)
        return other > z if kind == 0 else other < z

    def z_takes(kind, d):
        src = lax.rem(z + NZ - d, NZ)
        return src < z if kind == 0 else src > z

    def z_copy(kind, d):
        return pltpu.make_async_remote_copy(
            src_ref=zsend.at[kind],
            dst_ref=zrecv.at[d - 1],
            send_sem=z_send,
            recv_sem=z_recv.at[d - 1],
            device_id=(lax.rem(z + d, NZ) * PLANE + me, core),
            device_id_type=MESH,
        )

    def back_part(chip_pair, from_pair):
        return lax.div(lax.rem(from_pair - chip_pair + OWN, OWN), GROUP)

    def back_copy(kind, i):
        return pltpu.make_async_remote_copy(
            src_ref=send3.at[kind, i],
            dst_ref=recv3.at[kind, me],
            send_sem=s3_send.at[kind],
            recv_sem=s3_recv.at[kind, back_part(lax.div(i, 2), pair)],
            device_id=chip(i),
            device_id_type=MESH,
        )

    def give_back(kind):
        for d in range(1, NZ):

            @pl.when(z_takes(kind, d))
            def _():
                z_copy(kind, d).wait_recv()

        z_total[...] = jnp.zeros((HALF, DH), jnp.float32)
        for d in range(1, NZ):

            @pl.when(z_takes(kind, d))
            def _():
                diff = lax.rem(z + NZ - d, NZ) ^ z
                w = lax.select(diff >= 4, weight(9), lax.select(diff >= 2, weight(8), weight(7)))
                z_total[...] = z_total[...] + decode(zrecv[d - 1]) * w

        total = z_total[...]

        for i in BACK_ORDER:
            send3[kind, i] = encode(plane_buf[kind, i] + total)

            @pl.when(i != me)
            def _():
                back_copy(kind, i).start()

        recv3[kind, me] = send3[kind, me]

    def start_extra():
        def step(j, _):
            to_extra[j] = encode(sums[core, j])
            return 0

        lax.fori_loop(0, OWN, step, 0)
        extra.start()

    low = z < NZ // 2
    high = z >= NZ // 2

    def in_order(step):
        @pl.when(low)
        def _():
            step(0)
            step(1)

        @pl.when(high)
        def _():
            step(1)
            step(0)

    local(0, SPLIT_A)
    send_plane(0, 0)
    send_plane(0, 1)
    keep_plane(0)
    start_extra()
    local(SPLIT_A, SPLIT_B)
    combine(1)
    local(SPLIT_B, HEADS)
    combine(0)
    in_order(give_back)

    def forward(kind, j):
        slots = pl.ds(2 * j, 2)
        return pltpu.make_async_remote_copy(
            src_ref=recv3.at[kind, slots],
            dst_ref=fwd3.at[kind, slots],
            send_sem=f_send.at[kind],
            recv_sem=f_recv.at[kind, back_part(pair, j)],
            device_id=sibling,
            device_id_type=MESH,
        )

    def drain_early():
        extra.wait_send()
        drain(zrecv, z_send)
        for kind in range(2):
            drain(to_sibling.at[kind], d_send.at[kind])
            drain(send1.at[kind, pl.ds(0, PLANE - 1)], s1_send.at[kind])

    drain_early()
    up = lax.select(core == 1, 1.0, 0.0)
    dn = 1.0 - up

    def level2(kind, h):
        return lw[h, 2] * LEVEL_C[2] * (up if kind == 0 else dn)

    def make_base():
        def step(j, _):
            h = (1 - core) * OWN + j
            base_x[j] = level2(1, h) * decode(from_core_x[j])
            return 0

        lax.fori_loop(0, OWN, step, 0)

    extra.wait_recv()
    make_base()
    def finish(kind, heads, crosses):
        values = []
        for h, cross in zip(heads, crosses):
            c = cols(h)
            hi, lo = split(cross)
            stack = jnp.concatenate([hi, lo], axis=0)
            if kind == 0:
                ob = os_[:, c]
                more = dot_nn(jnp.concatenate([ob, ob], axis=1), stack)
                values.append((out_q, c, part_q[:, c] + more))
            else:
                vb, kb = vs[:, c], ks[:, c]
                wide = jnp.concatenate([hi, lo], axis=1)
                more = dot_nt(jnp.concatenate([vb, vb], axis=1), wide)
                values.append((out_k, c, part_k[:, c] + more))
                more = dot_nn(jnp.concatenate([kb, kb], axis=1), stack)
                values.append((out_v, c, part_v[:, c] + more))
        for ref, c, value in values:
            ref[:, c] = value.astype(jnp.bfloat16)

    def whole(buf, kind, j):
        return decode(jnp.concatenate([buf[kind, 2 * j], buf[kind, 2 * j + 1]], axis=0))

    def back_group(g):
        return [lax.rem(pair + g * GROUP + n, OWN) for n in range(GROUP)]

    def pass_on(kind):
        for g in range(OWN // GROUP):
            slots = 2 * GROUP - (1 if g == 0 else 0)
            drain(recv3.at[kind, pl.ds(0, slots)], s3_recv.at[kind, g])
            for j in back_group(g):
                forward(kind, j).start()

    def own_heads(kind):
        def step(g, _):
            slots = back_group(g)
            heads = [core * OWN + j for j in slots]
            finish(
                kind,
                heads,
                [
                    whole(recv3, kind, j) + level2(kind, h) * decode(from_core[kind, j])
                    for j, h in zip(slots, heads)
                ],
            )
            return 0

        lax.fori_loop(0, OWN // GROUP, step, 0)

    def other_heads(kind):
        for g in range(OWN // GROUP):
            slots = back_group(g)
            drain(fwd3.at[kind, pl.ds(0, 2 * GROUP)], f_recv.at[kind, g])
            heads = [(1 - core) * OWN + j for j in slots]
            finish(
                kind,
                heads,
                [
                    whole(fwd3, kind, j) + level2(kind, h) * decode(from_core_x[j])
                    for j, h in zip(slots, heads)
                ],
            )

    def drain_late():
        for g in range(OWN // GROUP):
            drain(fwd3.at[1, pl.ds(0, 2 * GROUP)], f_recv.at[1, g])
        for kind in range(2):
            drain(send3.at[kind, pl.ds(0, PLANE - 1)], s3_send.at[kind])
            drain(fwd3.at[kind], f_send.at[kind])

    def finish_all(kind):
        pass_on(kind)
        own_heads(kind)
        if kind == 0:
            other_heads(kind)

    in_order(finish_all)
    drain_late()


def store(
    out_q, out_k, out_v, fwd3, base_x, part_k, part_v, ks, vs, q_hbm, k_hbm, v_hbm,
    more_k, more_v, sem,
):
    core = lax.axis_index("head")
    width = OWN * DH
    own = pl.ds(pl.multiple_of(core * width, width), width)
    part = TOK // STORE_PARTS
    for p in range(STORE_PARTS):
        rows = pl.ds(p * part, part)
        pltpu.make_async_copy(out_k.at[rows, own], k_hbm.at[rows, own], sem.at[1]).start()
        pltpu.make_async_copy(out_v.at[rows, own], v_hbm.at[rows, own], sem.at[2]).start()
        pltpu.make_async_copy(out_q.at[rows], q_hbm.at[rows], sem.at[0]).start()
    for g in range(OWN // GROUP):
        values = []
        for j in range(g * GROUP, (g + 1) * GROUP):
            c = pl.ds(pl.multiple_of((1 - core) * width + j * DH, DH), DH)
            coded = jnp.concatenate([fwd3[1, 2 * j], fwd3[1, 2 * j + 1]], axis=0)
            hi, lo = split(decode(coded) + base_x[j])
            vb, kb = vs[:, c], ks[:, c]
            wide = jnp.concatenate([hi, lo], axis=1)
            stack = jnp.concatenate([hi, lo], axis=0)
            k_more = dot_nt(jnp.concatenate([vb, vb], axis=1), wide)
            v_more = dot_nn(jnp.concatenate([kb, kb], axis=1), stack)
            values.append((j, part_k[:, c] + k_more, part_v[:, c] + v_more))
        for j, k_new, v_new in values:
            more_k[:, j * DH : (j + 1) * DH] = k_new.astype(jnp.bfloat16)
            more_v[:, j * DH : (j + 1) * DH] = v_new.astype(jnp.bfloat16)
        size = GROUP * DH
        here = pl.ds(g * size, size)
        there = pl.ds(pl.multiple_of((1 - core) * width + g * size, size), size)
        for p in range(2):
            rows = pl.ds(p * BLOCK, BLOCK)
            pltpu.make_async_copy(more_k.at[rows, here], k_hbm.at[rows, there], sem.at[1]).start()
            pltpu.make_async_copy(more_v.at[rows, here], v_hbm.at[rows, there], sem.at[2]).start()
    for n, ref in enumerate((out_q, out_k, out_v)):
        pltpu.make_async_copy(ref, ref, sem.at[n]).wait()


def body(queries, key_rows, values, out_grad, level_weights):
    hbm = pl.BlockSpec(memory_space=pltpu.HBM)
    vmem = pl.BlockSpec(memory_space=pltpu.VMEM)
    bf, f32 = jnp.bfloat16, jnp.float32
    dma = pltpu.SemaphoreType.DMA
    rows = (TOK, HEADS * DH)
    out = jax.ShapeDtypeStruct(rows, bf)
    pinned = [
        pltpu.with_memory_space_constraint(a, pltpu.HBM)
        for a in (level_weights, queries, key_rows, values, out_grad)
    ]
    grads = pl.pallas_call(
        kernel,
        name="fenwick",
        out_shape=(pltpu.VMEM(rows, bf),) * 3
        + (
            pltpu.VMEM((2, PLANE, HALF, DH), bf),
            pltpu.VMEM((OWN, DH, DH), f32),
            pltpu.VMEM(rows, f32),
            pltpu.VMEM(rows, f32),
            pltpu.VMEM(rows, bf),
            pltpu.VMEM(rows, bf),
        ),
        in_specs=[hbm] * 5,
        out_specs=(vmem,) * 9,
        scratch_shapes=[pltpu.SMEM((HEADS, 11), f32)]
        + [pltpu.VMEM(rows, bf)] * 2
        + [
            pltpu.VMEM((2, OWN, DH, DH), f32),
            pltpu.VMEM((2, OWN, DH, DH), bf),
            pltpu.VMEM((OWN, DH, DH), bf),
            pltpu.VMEM((2, OWN, DH, DH), bf),
            pltpu.VMEM((OWN, DH, DH), bf),
            pltpu.VMEM((2, PLANE, HALF, DH), bf),
            pltpu.VMEM((2, PLANE, HALF, DH), bf),
            pltpu.VMEM((2, HALF, DH), bf),
            pltpu.VMEM((NZ - 1, HALF, DH), bf),
            pltpu.VMEM((HALF, DH), f32),
            pltpu.VMEM((2, PLANE, HALF, DH), bf),
            pltpu.VMEM((2, PLANE, HALF, DH), bf),
            pltpu.VMEM((2, PLANE, HALF, DH), f32),
        ]
        + [pltpu.VMEM(rows, f32)]
        + [
            dma((5,)),
            dma((2,)),
            dma((2, OWN // GROUP)),
            dma,
            dma,
            pltpu.SemaphoreType.REGULAR,
            dma((2,)),
            dma((2,)),
            dma,
            dma((NZ - 1,)),
            dma((2,)),
            dma((2, OWN // GROUP)),
            dma((2,)),
            dma((2, OWN // GROUP)),
        ],
        compiler_params=pltpu.CompilerParams(
            collective_id=0, has_side_effects=True, vmem_limit_bytes=40 << 20
        ),
    )(*pinned)
    return tuple(
        pl.pallas_call(
            store,
            name="store",
            out_shape=(out, out, out),
            in_specs=[vmem] * 9,
            out_specs=(hbm,) * 3,
            scratch_shapes=[pltpu.VMEM((TOK, OWN * DH), bf)] * 2 + [dma((3,))],
            compiler_params=pltpu.CompilerParams(vmem_limit_bytes=8 << 20),
        )(*(pltpu.with_memory_space_constraint(g, pltpu.VMEM) for g in grads))
    )


def solution(mesh):
    rows = P(("seq", "head"), None)
    return jax.shard_map(
        body,
        mesh=mesh,
        in_specs=(rows, rows, rows, rows, P()),
        out_specs=(rows, rows, rows),
        check_vma=False,
    )
```

```python
import functools

import jax
import jax.numpy as jnp
from jax import lax
from jax.experimental import pallas as pl
from jax.experimental.pallas import tpu as pltpu
from jax.sharding import PartitionSpec as P

DH = 128
BLOCK = 128
NX, NY, NZ = 4, 4, 8
PLANE = NX * NY
HEAD_ORDER = (5, 4, 3, 7, 2, 6, 1, 0)
BACK_ORDER = sorted(
    range(PLANE), key=lambda i: (min(i % NX, NX - i % NX) + min(i // NX, NY - i // NX), i)
)
HEADS = 16
OWN = HEADS // 2
HALF = DH // 2
TOK = 256
MESH = pl.DeviceIdType.MESH
GROUP = 4
LOCAL_GROUP = 2
SPLIT_A, SPLIT_B = 8, 8
LOAD_PARTS = 2
STORE_PARTS = 4
PRE = float(2.0**40)
POST = float(2.0**-40)
LEVEL_C = [float(2.0 ** ((1.0 - l) / 2.0) / 128.0) for l in range(11)]


def encode(x):
    s = x * PRE
    return (s * jnp.abs(s)).astype(jnp.bfloat16)


def decode(y):
    y = y.astype(jnp.float32)
    return y * (lax.rsqrt(jnp.maximum(jnp.abs(y), 1e-37)) * POST)


def dot_nn(a, b):
    return lax.dot_general(a, b, (((1,), (0,)), ((), ())), preferred_element_type=jnp.float32)


def dot_nt(a, b):
    return lax.dot_general(a, b, (((1,), (1,)), ((), ())), preferred_element_type=jnp.float32)


def dot_tn(a, b):
    return lax.dot_general(a, b, (((0,), (0,)), ((), ())), preferred_element_type=jnp.float32)


def split(x):
    hi = x.astype(jnp.bfloat16)
    lo = (x - hi.astype(jnp.float32)).astype(jnp.bfloat16)
    return hi, lo


def kernel(
    lw_hbm, q_hbm, k_hbm, v_hbm, o_hbm,
    out_q, out_k, out_v, fwd3, base_x, part_k, part_v, ks, vs,
    lw, qs, os_, sums, to_sibling, to_extra, from_core, from_core_x,
    send1, recv1, zsend, zrecv, z_total, send3, recv3, plane_buf, part_q,
    in_sem, d_send, d_recv, x_send, x_recv, z_ready, s1_send, s1_recv, z_send, z_recv,
    s3_send, s3_recv, f_send, f_recv,
):
    seq = lax.axis_index("seq")
    core = lax.axis_index("head")
    x = lax.rem(seq, NX)
    y = lax.rem(lax.div(seq, NX), NY)
    z = lax.div(seq, PLANE)
    me = y * NX + x
    pair = lax.div(me, 2)
    sibling = (seq, 1 - core)

    def chip(i):
        return (z * PLANE + i, core)

    width = OWN * DH
    loads = []
    stages = [(arrays, owner) for arrays in ("qo", "kv") for owner in (1 - core, core)]
    where = dict(q=(q_hbm, qs), k=(k_hbm, ks), v=(v_hbm, vs), o=(o_hbm, os_))
    for n, (arrays, owner) in enumerate(stages):
        half = pl.ds(pl.multiple_of(owner * width, width), width)
        loads.append([])
        for array in arrays:
            src, dst = where[array]
            for p in range(LOAD_PARTS):
                rows = pl.ds(p * (TOK // LOAD_PARTS), TOK // LOAD_PARTS)
                loads[n].append(
                    pltpu.make_async_copy(src.at[rows, half], dst.at[rows, half], in_sem.at[n])
                )
    loads.append([pltpu.make_async_copy(lw_hbm, lw, in_sem.at[4])])

    def start_loads(lo, hi):
        for stage in loads[lo:hi]:
            for c in stage:
                c.start()

    def wait_loads(n):
        if n < 4:
            drain(qs, in_sem.at[n])
        else:
            loads[n][0].wait()

    barrier = pltpu.get_barrier_semaphore()
    pl.semaphore_signal(barrier, inc=1, device_id=sibling, device_id_type=MESH)
    for d in (10, 6, 9, 11, 14, 2, 8, 5, 7, 13, 15, 1, 3, 4, 12):
        pl.semaphore_signal(
            barrier, inc=1, device_id=chip(lax.rem(me + d, PLANE)), device_id_type=MESH
        )
    for d in range(1, NZ):
        other = lax.rem(z + d, NZ)

        @pl.when(other > z)
        def _():
            pl.semaphore_signal(
                barrier, inc=1, device_id=(other * PLANE + me, core), device_id_type=MESH
            )

    start_loads(0, 2)

    def wait_barrier():
        pl.semaphore_wait(barrier, PLANE + z)
        for d in range(1, NZ):
            other = lax.rem(z + d, NZ)

            @pl.when(other < z)
            def _():
                pl.semaphore_signal(
                    z_ready, inc=1, device_id=(other * PLANE + me, core), device_id_type=MESH
                )

    def drain(buf, sem):
        pltpu.make_async_copy(buf, buf, sem).wait()

    def cols(h):
        return pl.ds(pl.multiple_of(h * DH, DH), DH)

    def states(kind, h):
        a, b = (vs, ks) if kind == 0 else (qs, os_)
        c = cols(h)
        return dot_tn(a[:, c], b[:, c])

    def part(j):
        return HEAD_ORDER.index(j) // GROUP

    def to_core(kind, j):
        return pltpu.make_async_remote_copy(
            src_ref=to_sibling.at[kind, j],
            dst_ref=from_core.at[kind, j],
            send_sem=d_send.at[kind],
            recv_sem=d_recv.at[kind, part(j)],
            device_id=sibling,
            device_id_type=MESH,
        )

    def group(g):
        return HEAD_ORDER[g * GROUP : (g + 1) * GROUP]

    def states_for_sibling(kind, g):
        values = [states(kind, (1 - core) * OWN + j) for j in group(g)]
        for j, value in zip(group(g), values):
            to_sibling[kind, j] = encode(value)

    def send_core(kind, g):
        for j in group(g):
            to_core(kind, j).start()

    def states_own(kind, g):
        values = [states(kind, core * OWN + j) for j in group(g)]
        for j, value in zip(group(g), values):
            sums[kind, j] = value

    def plane_copy(kind, i):
        return pltpu.make_async_remote_copy(
            src_ref=send1.at[kind, i],
            dst_ref=recv1.at[kind, me],
            send_sem=s1_send.at[kind],
            recv_sem=s1_recv.at[kind],
            device_id=chip(i),
            device_id_type=MESH,
        )

    def send_plane(kind, g):
        drain(from_core.at[kind, pl.ds(0, GROUP)], d_recv.at[kind, g])
        for j in group(g):
            for half in range(2):
                rows = pl.ds(half * HALF, HALF)
                total = sums[kind, j, rows] + decode(from_core[kind, j, rows])
                send1[kind, 2 * j + half] = encode(total)
        for j in group(g):
            for half in range(2):
                i = 2 * j + half

                @pl.when(i != me)
                def _():
                    plane_copy(kind, i).start()

    def keep_plane(kind):
        recv1[kind, me] = send1[kind, me]

    wait_loads(0)
    start_loads(2, 5)
    states_for_sibling(1, 0)
    states_for_sibling(1, 1)
    wait_loads(1)
    states_own(1, 0)
    wait_barrier()
    send_core(1, 0)
    send_core(1, 1)
    states_own(1, 1)
    send_plane(1, 0)
    send_plane(1, 1)
    keep_plane(1)
    wait_loads(2)
    states_for_sibling(0, 0)
    send_core(0, 0)
    states_for_sibling(0, 1)
    send_core(0, 1)
    wait_loads(3)
    states_own(0, 0)
    states_own(0, 1)
    wait_loads(4)

    row = lax.broadcasted_iota(jnp.int32, (BLOCK, BLOCK), 0)
    col = lax.broadcasted_iota(jnp.int32, (BLOCK, BLOCK), 1)
    lower = row >= col
    upper = row <= col

    A, B = slice(0, BLOCK), slice(BLOCK, TOK)

    def local_heads(first_head):
        heads = [first_head + n for n in range(LOCAL_GROUP)]
        data = []
        for h in heads:
            c = cols(h)
            data.append((qs[:, c], ks[:, c], vs[:, c], os_[:, c]))
        scores = []
        for qb, kb, vb, ob in data:
            scores.append(
                (
                    dot_nt(ob[A], vb[A]), dot_nt(ob[B], vb),
                    dot_nt(vb[A], ob), dot_nt(vb[B], ob[B]),
                    dot_nt(kb[A], qb), dot_nt(kb[B], qb[B]),
                )
            )
        weighted = []
        for h, (g_a, g_b, gt_a, gt_b, wt_a, wt_b) in zip(heads, scores):
            w0 = lw[h, 0] * LEVEL_C[0]
            w1 = lw[h, 1] * LEVEL_C[1]

            def masked(score, mask):
                return jnp.where(mask, score * w0, 0.0).astype(jnp.bfloat16)

            def level1(score):
                return (score * w1).astype(jnp.bfloat16)

            def join(a, b):
                return jnp.concatenate([a, b], axis=1)

            weighted.append(
                (
                    masked(g_a, lower), join(level1(g_b[:, A]), masked(g_b[:, B], lower)),
                    join(masked(gt_a[:, A], upper), level1(gt_a[:, B])), masked(gt_b, upper),
                    join(masked(wt_a[:, A], upper), level1(wt_a[:, B])), masked(wt_b, upper),
                )
            )
        results = []
        for (qb, kb, vb, ob), (g_a, g_b, gt_a, gt_b, wt_a, wt_b) in zip(data, weighted):
            results.append(
                (
                    dot_nn(g_a, kb[A]), dot_nn(g_b, kb),
                    dot_nn(gt_a, qb), dot_nn(gt_b, qb[B]),
                    dot_nn(wt_a, ob), dot_nn(wt_b, ob[B]),
                )
            )
        for h, values in zip(heads, results):
            c = cols(h)
            for n, part in enumerate((part_q, part_k, part_v)):
                part[A, c] = values[2 * n]
                part[B, c] = values[2 * n + 1]

    def local(lo, hi):
        def step(n, _):
            local_heads(lo + n * LOCAL_GROUP)
            return 0

        lax.fori_loop(0, (hi - lo) // LOCAL_GROUP, step, 0)

    extra = pltpu.make_async_remote_copy(
        src_ref=to_extra,
        dst_ref=from_core_x,
        send_sem=x_send,
        recv_sem=x_recv,
        device_id=sibling,
        device_id_type=MESH,
    )

    hs = core * OWN + pair

    def weight(level):
        return lw[hs, level] * LEVEL_C[level]

    def combine(kind):
        others = pl.ds(0, PLANE - 1)
        pltpu.make_async_copy(
            recv1.at[kind, others], recv1.at[kind, others], s1_recv.at[kind]
        ).wait()
        nodes = [decode(recv1[kind, i]) for i in range(PLANE)]
        tree = [nodes]
        while len(tree[-1]) > 1:
            last = tree[-1]
            tree.append([last[n] + last[n + 1] for n in range(0, len(last), 2)])
        zsend[kind] = encode(tree[-1][0])
        if kind == 0:

            @pl.when(z < NZ - 1)
            def _():
                pl.semaphore_wait(z_ready, NZ - 1 - z)

        for d in range(1, NZ):

            @pl.when(z_sends(kind, d))
            def _():
                z_copy(kind, d).start()

        down = [None]
        for level in range(len(tree) - 2, -1, -1):
            w = weight(3 + level)
            new = []
            for n, parent in enumerate(down):
                a, b = tree[level][2 * n], tree[level][2 * n + 1]
                from_a, from_b = parent, parent
                if kind == 0:
                    from_b = a * w if parent is None else parent + a * w
                else:
                    from_a = b * w if parent is None else parent + b * w
                new += [from_a, from_b]
            down = new
        for i in range(PLANE):
            value = down[i]
            plane_buf[kind, i] = jnp.zeros((HALF, DH), jnp.float32) if value is None else value

    def z_sends(kind, d):
        other = lax.rem(z + d, NZ)
        return other > z if kind == 0 else other < z

    def z_takes(kind, d):
        src = lax.rem(z + NZ - d, NZ)
        return src < z if kind == 0 else src > z

    def z_copy(kind, d):
        return pltpu.make_async_remote_copy(
            src_ref=zsend.at[kind],
            dst_ref=zrecv.at[d - 1],
            send_sem=z_send,
            recv_sem=z_recv.at[d - 1],
            device_id=(lax.rem(z + d, NZ) * PLANE + me, core),
            device_id_type=MESH,
        )

    def back_part(chip_pair, from_pair):
        return lax.div(lax.rem(from_pair - chip_pair + OWN, OWN), GROUP)

    def back_copy(kind, i):
        return pltpu.make_async_remote_copy(
            src_ref=send3.at[kind, i],
            dst_ref=recv3.at[kind, me],
            send_sem=s3_send.at[kind],
            recv_sem=s3_recv.at[kind, back_part(lax.div(i, 2), pair)],
            device_id=chip(i),
            device_id_type=MESH,
        )

    def give_back(kind):
        for d in range(1, NZ):

            @pl.when(z_takes(kind, d))
            def _():
                z_copy(kind, d).wait_recv()

        z_total[...] = jnp.zeros((HALF, DH), jnp.float32)
        for d in range(1, NZ):

            @pl.when(z_takes(kind, d))
            def _():
                diff = lax.rem(z + NZ - d, NZ) ^ z
                w = lax.select(diff >= 4, weight(9), lax.select(diff >= 2, weight(8), weight(7)))
                z_total[...] = z_total[...] + decode(zrecv[d - 1]) * w

        total = z_total[...]

        for i in BACK_ORDER:
            send3[kind, i] = encode(plane_buf[kind, i] + total)

            @pl.when(i != me)
            def _():
                back_copy(kind, i).start()

        recv3[kind, me] = send3[kind, me]

    def start_extra():
        def step(j, _):
            to_extra[j] = encode(sums[core, j])
            return 0

        lax.fori_loop(0, OWN, step, 0)
        extra.start()

    low = z < NZ // 2
    high = z >= NZ // 2

    def in_order(step):
        @pl.when(low)
        def _():
            step(0)
            step(1)

        @pl.when(high)
        def _():
            step(1)
            step(0)

    local(0, SPLIT_A)
    send_plane(0, 0)
    send_plane(0, 1)
    keep_plane(0)
    start_extra()
    local(SPLIT_A, SPLIT_B)
    combine(1)
    local(SPLIT_B, HEADS)
    combine(0)
    in_order(give_back)

    def forward(kind, j):
        slots = pl.ds(2 * j, 2)
        return pltpu.make_async_remote_copy(
            src_ref=recv3.at[kind, slots],
            dst_ref=fwd3.at[kind, slots],
            send_sem=f_send.at[kind],
            recv_sem=f_recv.at[kind, back_part(pair, j)],
            device_id=sibling,
            device_id_type=MESH,
        )

    def drain_early():
        extra.wait_send()
        drain(zrecv, z_send)
        for kind in range(2):
            drain(to_sibling.at[kind], d_send.at[kind])
            drain(send1.at[kind, pl.ds(0, PLANE - 1)], s1_send.at[kind])

    drain_early()
    up = lax.select(core == 1, 1.0, 0.0)
    dn = 1.0 - up

    def level2(kind, h):
        return lw[h, 2] * LEVEL_C[2] * (up if kind == 0 else dn)

    def make_base():
        def step(j, _):
            h = (1 - core) * OWN + j
            base_x[j] = level2(1, h) * decode(from_core_x[j])
            return 0

        lax.fori_loop(0, OWN, step, 0)

    extra.wait_recv()
    make_base()
    def finish(kind, heads, crosses):
        values = []
        for h, cross in zip(heads, crosses):
            c = cols(h)
            hi, lo = split(cross)
            stack = jnp.concatenate([hi, lo], axis=0)
            if kind == 0:
                ob = os_[:, c]
                more = dot_nn(jnp.concatenate([ob, ob], axis=1), stack)
                values.append((out_q, c, part_q[:, c] + more))
            else:
                vb, kb = vs[:, c], ks[:, c]
                wide = jnp.concatenate([hi, lo], axis=1)
                more = dot_nt(jnp.concatenate([vb, vb], axis=1), wide)
                values.append((out_k, c, part_k[:, c] + more))
                more = dot_nn(jnp.concatenate([kb, kb], axis=1), stack)
                values.append((out_v, c, part_v[:, c] + more))
        for ref, c, value in values:
            ref[:, c] = value.astype(jnp.bfloat16)

    def whole(buf, kind, j):
        return decode(jnp.concatenate([buf[kind, 2 * j], buf[kind, 2 * j + 1]], axis=0))

    def back_group(g):
        return [lax.rem(pair + g * GROUP + n, OWN) for n in range(GROUP)]

    def pass_on(kind):
        for g in range(OWN // GROUP):
            slots = 2 * GROUP - (1 if g == 0 else 0)
            drain(recv3.at[kind, pl.ds(0, slots)], s3_recv.at[kind, g])
            for j in back_group(g):
                forward(kind, j).start()

    def own_heads(kind):
        def step(g, _):
            slots = back_group(g)
            heads = [core * OWN + j for j in slots]
            finish(
                kind,
                heads,
                [
                    whole(recv3, kind, j) + level2(kind, h) * decode(from_core[kind, j])
                    for j, h in zip(slots, heads)
                ],
            )
            return 0

        lax.fori_loop(0, OWN // GROUP, step, 0)

    def other_heads(kind):
        for g in range(OWN // GROUP):
            slots = back_group(g)
            drain(fwd3.at[kind, pl.ds(0, 2 * GROUP)], f_recv.at[kind, g])
            heads = [(1 - core) * OWN + j for j in slots]
            finish(
                kind,
                heads,
                [
                    whole(fwd3, kind, j) + level2(kind, h) * decode(from_core_x[j])
                    for j, h in zip(slots, heads)
                ],
            )

    def drain_late():
        for g in range(OWN // GROUP):
            drain(fwd3.at[1, pl.ds(0, 2 * GROUP)], f_recv.at[1, g])
        for kind in range(2):
            drain(send3.at[kind, pl.ds(0, PLANE - 1)], s3_send.at[kind])
            drain(fwd3.at[kind], f_send.at[kind])

    def finish_all(kind):
        pass_on(kind)
        own_heads(kind)
        if kind == 0:
            other_heads(kind)

    in_order(finish_all)
    drain_late()


def store(
    out_q, out_k, out_v, fwd3, base_x, part_k, part_v, ks, vs, q_hbm, k_hbm, v_hbm,
    more_k, more_v, sem,
):
    core = lax.axis_index("head")
    width = OWN * DH
    own = pl.ds(pl.multiple_of(core * width, width), width)
    part = TOK // STORE_PARTS
    for p in range(STORE_PARTS):
        rows = pl.ds(p * part, part)
        pltpu.make_async_copy(out_k.at[rows, own], k_hbm.at[rows, own], sem.at[1]).start()
        pltpu.make_async_copy(out_v.at[rows, own], v_hbm.at[rows, own], sem.at[2]).start()
        pltpu.make_async_copy(out_q.at[rows], q_hbm.at[rows], sem.at[0]).start()
    for g in range(OWN // GROUP):
        values = []
        for j in range(g * GROUP, (g + 1) * GROUP):
            c = pl.ds(pl.multiple_of((1 - core) * width + j * DH, DH), DH)
            coded = jnp.concatenate([fwd3[1, 2 * j], fwd3[1, 2 * j + 1]], axis=0)
            hi, lo = split(decode(coded) + base_x[j])
            vb, kb = vs[:, c], ks[:, c]
            wide = jnp.concatenate([hi, lo], axis=1)
            stack = jnp.concatenate([hi, lo], axis=0)
            k_more = dot_nt(jnp.concatenate([vb, vb], axis=1), wide)
            v_more = dot_nn(jnp.concatenate([kb, kb], axis=1), stack)
            values.append((j, part_k[:, c] + k_more, part_v[:, c] + v_more))
        for j, k_new, v_new in values:
            more_k[:, j * DH : (j + 1) * DH] = k_new.astype(jnp.bfloat16)
            more_v[:, j * DH : (j + 1) * DH] = v_new.astype(jnp.bfloat16)
        size = GROUP * DH
        here = pl.ds(g * size, size)
        there = pl.ds(pl.multiple_of((1 - core) * width + g * size, size), size)
        for p in range(2):
            rows = pl.ds(p * BLOCK, BLOCK)
            pltpu.make_async_copy(more_k.at[rows, here], k_hbm.at[rows, there], sem.at[1]).start()
            pltpu.make_async_copy(more_v.at[rows, here], v_hbm.at[rows, there], sem.at[2]).start()
    for n, ref in enumerate((out_q, out_k, out_v)):
        pltpu.make_async_copy(ref, ref, sem.at[n]).wait()


def body(queries, key_rows, values, out_grad, level_weights):
    hbm = pl.BlockSpec(memory_space=pltpu.HBM)
    vmem = pl.BlockSpec(memory_space=pltpu.VMEM)
    bf, f32 = jnp.bfloat16, jnp.float32
    dma = pltpu.SemaphoreType.DMA
    rows = (TOK, HEADS * DH)
    out = jax.ShapeDtypeStruct(rows, bf)
    pinned = [
        pltpu.with_memory_space_constraint(a, pltpu.HBM)
        for a in (level_weights, queries, key_rows, values, out_grad)
    ]
    grads = pl.pallas_call(
        kernel,
        name="fenwick",
        out_shape=(pltpu.VMEM(rows, bf),) * 3
        + (
            pltpu.VMEM((2, PLANE, HALF, DH), bf),
            pltpu.VMEM((OWN, DH, DH), f32),
            pltpu.VMEM(rows, f32),
            pltpu.VMEM(rows, f32),
            pltpu.VMEM(rows, bf),
            pltpu.VMEM(rows, bf),
        ),
        in_specs=[hbm] * 5,
        out_specs=(vmem,) * 9,
        scratch_shapes=[pltpu.SMEM((HEADS, 11), f32)]
        + [pltpu.VMEM(rows, bf)] * 2
        + [
            pltpu.VMEM((2, OWN, DH, DH), f32),
            pltpu.VMEM((2, OWN, DH, DH), bf),
            pltpu.VMEM((OWN, DH, DH), bf),
            pltpu.VMEM((2, OWN, DH, DH), bf),
            pltpu.VMEM((OWN, DH, DH), bf),
            pltpu.VMEM((2, PLANE, HALF, DH), bf),
            pltpu.VMEM((2, PLANE, HALF, DH), bf),
            pltpu.VMEM((2, HALF, DH), bf),
            pltpu.VMEM((NZ - 1, HALF, DH), bf),
            pltpu.VMEM((HALF, DH), f32),
            pltpu.VMEM((2, PLANE, HALF, DH), bf),
            pltpu.VMEM((2, PLANE, HALF, DH), bf),
            pltpu.VMEM((2, PLANE, HALF, DH), f32),
        ]
        + [pltpu.VMEM(rows, f32)]
        + [
            dma((5,)),
            dma((2,)),
            dma((2, OWN // GROUP)),
            dma,
            dma,
            pltpu.SemaphoreType.REGULAR,
            dma((2,)),
            dma((2,)),
            dma,
            dma((NZ - 1,)),
            dma((2,)),
            dma((2, OWN // GROUP)),
            dma((2,)),
            dma((2, OWN // GROUP)),
        ],
        compiler_params=pltpu.CompilerParams(
            collective_id=0, has_side_effects=True, vmem_limit_bytes=40 << 20
        ),
    )(*pinned)
    return tuple(
        pl.pallas_call(
            store,
            name="store",
            out_shape=(out, out, out),
            in_specs=[vmem] * 9,
            out_specs=(hbm,) * 3,
            scratch_shapes=[pltpu.VMEM((TOK, OWN * DH), bf)] * 2 + [dma((3,))],
            compiler_params=pltpu.CompilerParams(vmem_limit_bytes=8 << 20),
        )(*(pltpu.with_memory_space_constraint(g, pltpu.VMEM) for g in grads))
    )


def solution(mesh):
    rows = P(("seq", "head"), None)
    return jax.shard_map(
        body,
        mesh=mesh,
        in_specs=(rows, rows, rows, rows, P()),
        out_specs=(rows, rows, rows),
        check_vma=False,
    )
```

```python
import functools

import jax
import jax.numpy as jnp
from jax import lax
from jax.experimental import pallas as pl
from jax.experimental.pallas import tpu as pltpu
from jax.sharding import PartitionSpec as P

DH = 128
BLOCK = 128
NX, NY, NZ = 4, 4, 8
PLANE = NX * NY
HEAD_ORDER = (5, 7, 3, 4, 2, 6, 1, 0)
BACK_ORDER = sorted(
    range(PLANE), key=lambda i: (min(i % NX, NX - i % NX) + min(i // NX, NY - i // NX), i)
)
HEADS = 16
OWN = HEADS // 2
HALF = DH // 2
TOK = 256
MESH = pl.DeviceIdType.MESH
GROUP = 4
LOCAL_GROUP = 2
SPLIT_A, SPLIT_B = 6, 6
LOAD_PARTS = 2
STORE_PARTS = 4
PRE = float(2.0**40)
POST = float(2.0**-40)
LEVEL_C = [float(2.0 ** ((1.0 - l) / 2.0) / 128.0) for l in range(11)]


def encode(x):
    s = x * PRE
    return (s * jnp.abs(s)).astype(jnp.bfloat16)


def decode(y):
    y = y.astype(jnp.float32)
    return y * (lax.rsqrt(jnp.maximum(jnp.abs(y), 1e-37)) * POST)


def dot_nn(a, b):
    return lax.dot_general(a, b, (((1,), (0,)), ((), ())), preferred_element_type=jnp.float32)


def dot_nt(a, b):
    return lax.dot_general(a, b, (((1,), (1,)), ((), ())), preferred_element_type=jnp.float32)


def dot_tn(a, b):
    return lax.dot_general(a, b, (((0,), (0,)), ((), ())), preferred_element_type=jnp.float32)


def split(x):
    hi = x.astype(jnp.bfloat16)
    lo = (x - hi.astype(jnp.float32)).astype(jnp.bfloat16)
    return hi, lo


def kernel(
    lw_hbm, q_hbm, k_hbm, v_hbm, o_hbm,
    out_q, out_k, out_v, fwd3, base_x, part_k, part_v, ks, vs,
    lw, qs, os_, sums, to_sibling, to_extra, from_core, from_core_x,
    send1, recv1, zsend, zrecv, z_total, send3, recv3, plane_buf, part_q,
    in_sem, d_send, d_recv, x_send, x_recv, z_ready, s1_send, s1_recv, z_send, z_recv,
    s3_send, s3_recv, f_send, f_recv,
):
    seq = lax.axis_index("seq")
    core = lax.axis_index("head")
    x = lax.rem(seq, NX)
    y = lax.rem(lax.div(seq, NX), NY)
    z = lax.div(seq, PLANE)
    me = y * NX + x
    pair = lax.div(me, 2)
    sibling = (seq, 1 - core)

    def chip(i):
        return (z * PLANE + i, core)

    width = OWN * DH
    loads = []
    stages = [(arrays, owner) for arrays in ("qo", "kv") for owner in (1 - core, core)]
    where = dict(q=(q_hbm, qs), k=(k_hbm, ks), v=(v_hbm, vs), o=(o_hbm, os_))
    for n, (arrays, owner) in enumerate(stages):
        half = pl.ds(pl.multiple_of(owner * width, width), width)
        loads.append([])
        for array in arrays:
            src, dst = where[array]
            for p in range(LOAD_PARTS):
                rows = pl.ds(p * (TOK // LOAD_PARTS), TOK // LOAD_PARTS)
                loads[n].append(
                    pltpu.make_async_copy(src.at[rows, half], dst.at[rows, half], in_sem.at[n])
                )
    loads.append([pltpu.make_async_copy(lw_hbm, lw, in_sem.at[4])])

    def start_loads(lo, hi):
        for stage in loads[lo:hi]:
            for c in stage:
                c.start()

    def wait_loads(n):
        if n < 4:
            drain(qs, in_sem.at[n])
        else:
            loads[n][0].wait()

    barrier = pltpu.get_barrier_semaphore()
    pl.semaphore_signal(barrier, inc=1, device_id=sibling, device_id_type=MESH)
    for d in (10, 6, 9, 11, 14, 2, 8, 5, 7, 13, 15, 1, 3, 4, 12):
        pl.semaphore_signal(
            barrier, inc=1, device_id=chip(lax.rem(me + d, PLANE)), device_id_type=MESH
        )
    for d in range(1, NZ):
        other = lax.rem(z + d, NZ)

        @pl.when(other > z)
        def _():
            pl.semaphore_signal(
                barrier, inc=1, device_id=(other * PLANE + me, core), device_id_type=MESH
            )

    start_loads(0, 2)

    def wait_barrier():
        pl.semaphore_wait(barrier, PLANE + z)
        for d in range(1, NZ):
            other = lax.rem(z + d, NZ)

            @pl.when(other < z)
            def _():
                pl.semaphore_signal(
                    z_ready, inc=1, device_id=(other * PLANE + me, core), device_id_type=MESH
                )

    def drain(buf, sem):
        pltpu.make_async_copy(buf, buf, sem).wait()

    def cols(h):
        return pl.ds(pl.multiple_of(h * DH, DH), DH)

    def states(kind, h):
        a, b = (vs, ks) if kind == 0 else (qs, os_)
        c = cols(h)
        return dot_tn(a[:, c], b[:, c])

    def part(j):
        return HEAD_ORDER.index(j) // GROUP

    def to_core(kind, j):
        return pltpu.make_async_remote_copy(
            src_ref=to_sibling.at[kind, j],
            dst_ref=from_core.at[kind, j],
            send_sem=d_send.at[kind],
            recv_sem=d_recv.at[kind, part(j)],
            device_id=sibling,
            device_id_type=MESH,
        )

    def group(g):
        return HEAD_ORDER[g * GROUP : (g + 1) * GROUP]

    def states_for_sibling(kind, g):
        values = [states(kind, (1 - core) * OWN + j) for j in group(g)]
        for j, value in zip(group(g), values):
            to_sibling[kind, j] = encode(value)

    def send_core(kind, g):
        for j in group(g):
            to_core(kind, j).start()

    def states_own(kind, g):
        values = [states(kind, core * OWN + j) for j in group(g)]
        for j, value in zip(group(g), values):
            sums[kind, j] = value

    def plane_copy(kind, i):
        return pltpu.make_async_remote_copy(
            src_ref=send1.at[kind, i],
            dst_ref=recv1.at[kind, me],
            send_sem=s1_send.at[kind],
            recv_sem=s1_recv.at[kind],
            device_id=chip(i),
            device_id_type=MESH,
        )

    def send_plane(kind, g):
        drain(from_core.at[kind, pl.ds(0, GROUP)], d_recv.at[kind, g])
        for j in group(g):
            for half in range(2):
                rows = pl.ds(half * HALF, HALF)
                total = sums[kind, j, rows] + decode(from_core[kind, j, rows])
                send1[kind, 2 * j + half] = encode(total)
        for j in group(g):
            for half in range(2):
                i = 2 * j + half

                @pl.when(i != me)
                def _():
                    plane_copy(kind, i).start()

    def keep_plane(kind):
        recv1[kind, me] = send1[kind, me]

    wait_loads(0)
    start_loads(2, 5)
    states_for_sibling(1, 0)
    states_for_sibling(1, 1)
    wait_loads(1)
    states_own(1, 0)
    wait_barrier()
    send_core(1, 0)
    send_core(1, 1)
    states_own(1, 1)
    send_plane(1, 0)
    send_plane(1, 1)
    keep_plane(1)
    wait_loads(2)
    states_for_sibling(0, 0)
    send_core(0, 0)
    states_for_sibling(0, 1)
    send_core(0, 1)
    wait_loads(3)
    states_own(0, 0)
    states_own(0, 1)
    wait_loads(4)

    row = lax.broadcasted_iota(jnp.int32, (BLOCK, BLOCK), 0)
    col = lax.broadcasted_iota(jnp.int32, (BLOCK, BLOCK), 1)
    lower = row >= col
    upper = row <= col

    A, B = slice(0, BLOCK), slice(BLOCK, TOK)

    def local_heads(first_head):
        heads = [first_head + n for n in range(LOCAL_GROUP)]
        data = []
        for h in heads:
            c = cols(h)
            data.append((qs[:, c], ks[:, c], vs[:, c], os_[:, c]))
        scores = []
        for qb, kb, vb, ob in data:
            scores.append(
                (
                    dot_nt(ob[A], vb[A]), dot_nt(ob[B], vb),
                    dot_nt(vb[A], ob), dot_nt(vb[B], ob[B]),
                    dot_nt(kb[A], qb), dot_nt(kb[B], qb[B]),
                )
            )
        weighted = []
        for h, (g_a, g_b, gt_a, gt_b, wt_a, wt_b) in zip(heads, scores):
            w0 = lw[h, 0] * LEVEL_C[0]
            w1 = lw[h, 1] * LEVEL_C[1]

            def masked(score, mask):
                return jnp.where(mask, score * w0, 0.0).astype(jnp.bfloat16)

            def level1(score):
                return (score * w1).astype(jnp.bfloat16)

            def join(a, b):
                return jnp.concatenate([a, b], axis=1)

            weighted.append(
                (
                    masked(g_a, lower), join(level1(g_b[:, A]), masked(g_b[:, B], lower)),
                    join(masked(gt_a[:, A], upper), level1(gt_a[:, B])), masked(gt_b, upper),
                    join(masked(wt_a[:, A], upper), level1(wt_a[:, B])), masked(wt_b, upper),
                )
            )
        results = []
        for (qb, kb, vb, ob), (g_a, g_b, gt_a, gt_b, wt_a, wt_b) in zip(data, weighted):
            results.append(
                (
                    dot_nn(g_a, kb[A]), dot_nn(g_b, kb),
                    dot_nn(gt_a, qb), dot_nn(gt_b, qb[B]),
                    dot_nn(wt_a, ob), dot_nn(wt_b, ob[B]),
                )
            )
        for h, values in zip(heads, results):
            c = cols(h)
            for n, part in enumerate((part_q, part_k, part_v)):
                part[A, c] = values[2 * n]
                part[B, c] = values[2 * n + 1]

    def local(lo, hi):
        def step(n, _):
            local_heads(lo + n * LOCAL_GROUP)
            return 0

        lax.fori_loop(0, (hi - lo) // LOCAL_GROUP, step, 0)

    extra = pltpu.make_async_remote_copy(
        src_ref=to_extra,
        dst_ref=from_core_x,
        send_sem=x_send,
        recv_sem=x_recv,
        device_id=sibling,
        device_id_type=MESH,
    )

    hs = core * OWN + pair

    def weight(level):
        return lw[hs, level] * LEVEL_C[level]

    def combine(kind):
        others = pl.ds(0, PLANE - 1)
        pltpu.make_async_copy(
            recv1.at[kind, others], recv1.at[kind, others], s1_recv.at[kind]
        ).wait()
        nodes = [decode(recv1[kind, i]) for i in range(PLANE)]
        tree = [nodes]
        while len(tree[-1]) > 1:
            last = tree[-1]
            tree.append([last[n] + last[n + 1] for n in range(0, len(last), 2)])
        zsend[kind] = encode(tree[-1][0])
        if kind == 0:

            @pl.when(z < NZ - 1)
            def _():
                pl.semaphore_wait(z_ready, NZ - 1 - z)

        for d in range(1, NZ):

            @pl.when(z_sends(kind, d))
            def _():
                z_copy(kind, d).start()

        down = [None]
        for level in range(len(tree) - 2, -1, -1):
            w = weight(3 + level)
            new = []
            for n, parent in enumerate(down):
                a, b = tree[level][2 * n], tree[level][2 * n + 1]
                from_a, from_b = parent, parent
                if kind == 0:
                    from_b = a * w if parent is None else parent + a * w
                else:
                    from_a = b * w if parent is None else parent + b * w
                new += [from_a, from_b]
            down = new
        for i in range(PLANE):
            value = down[i]
            plane_buf[kind, i] = jnp.zeros((HALF, DH), jnp.float32) if value is None else value

    def z_sends(kind, d):
        other = lax.rem(z + d, NZ)
        return other > z if kind == 0 else other < z

    def z_takes(kind, d):
        src = lax.rem(z + NZ - d, NZ)
        return src < z if kind == 0 else src > z

    def z_copy(kind, d):
        return pltpu.make_async_remote_copy(
            src_ref=zsend.at[kind],
            dst_ref=zrecv.at[d - 1],
            send_sem=z_send,
            recv_sem=z_recv.at[d - 1],
            device_id=(lax.rem(z + d, NZ) * PLANE + me, core),
            device_id_type=MESH,
        )

    def back_part(chip_pair, from_pair):
        return lax.div(lax.rem(from_pair - chip_pair + OWN, OWN), GROUP)

    def back_copy(kind, i):
        return pltpu.make_async_remote_copy(
            src_ref=send3.at[kind, i],
            dst_ref=recv3.at[kind, me],
            send_sem=s3_send.at[kind],
            recv_sem=s3_recv.at[kind, back_part(lax.div(i, 2), pair)],
            device_id=chip(i),
            device_id_type=MESH,
        )

    def give_back(kind):
        for d in range(1, NZ):

            @pl.when(z_takes(kind, d))
            def _():
                z_copy(kind, d).wait_recv()

        z_total[...] = jnp.zeros((HALF, DH), jnp.float32)
        for d in range(1, NZ):

            @pl.when(z_takes(kind, d))
            def _():
                diff = lax.rem(z + NZ - d, NZ) ^ z
                w = lax.select(diff >= 4, weight(9), lax.select(diff >= 2, weight(8), weight(7)))
                z_total[...] = z_total[...] + decode(zrecv[d - 1]) * w

        total = z_total[...]

        for i in BACK_ORDER:
            send3[kind, i] = encode(plane_buf[kind, i] + total)

            @pl.when(i != me)
            def _():
                back_copy(kind, i).start()

        recv3[kind, me] = send3[kind, me]

    def start_extra():
        def step(j, _):
            to_extra[j] = encode(sums[core, j])
            return 0

        lax.fori_loop(0, OWN, step, 0)
        extra.start()

    low = z < NZ // 2
    high = z >= NZ // 2

    def in_order(step):
        @pl.when(low)
        def _():
            step(0)
            step(1)

        @pl.when(high)
        def _():
            step(1)
            step(0)

    local(0, SPLIT_A)
    send_plane(0, 0)
    send_plane(0, 1)
    keep_plane(0)
    start_extra()
    local(SPLIT_A, SPLIT_B)
    combine(1)
    local(SPLIT_B, HEADS)
    combine(0)
    in_order(give_back)

    def forward(kind, j):
        slots = pl.ds(2 * j, 2)
        return pltpu.make_async_remote_copy(
            src_ref=recv3.at[kind, slots],
            dst_ref=fwd3.at[kind, slots],
            send_sem=f_send.at[kind],
            recv_sem=f_recv.at[kind, back_part(pair, j)],
            device_id=sibling,
            device_id_type=MESH,
        )

    def drain_early():
        extra.wait_send()
        drain(zrecv, z_send)
        for kind in range(2):
            drain(to_sibling.at[kind], d_send.at[kind])
            drain(send1.at[kind, pl.ds(0, PLANE - 1)], s1_send.at[kind])

    drain_early()
    up = lax.select(core == 1, 1.0, 0.0)
    dn = 1.0 - up

    def level2(kind, h):
        return lw[h, 2] * LEVEL_C[2] * (up if kind == 0 else dn)

    def make_base():
        def step(j, _):
            h = (1 - core) * OWN + j
            base_x[j] = level2(1, h) * decode(from_core_x[j])
            return 0

        lax.fori_loop(0, OWN, step, 0)

    extra.wait_recv()
    make_base()
    def finish(kind, heads, crosses):
        values = []
        for h, cross in zip(heads, crosses):
            c = cols(h)
            hi, lo = split(cross)
            stack = jnp.concatenate([hi, lo], axis=0)
            if kind == 0:
                ob = os_[:, c]
                more = dot_nn(jnp.concatenate([ob, ob], axis=1), stack)
                values.append((out_q, c, part_q[:, c] + more))
            else:
                vb, kb = vs[:, c], ks[:, c]
                wide = jnp.concatenate([hi, lo], axis=1)
                more = dot_nt(jnp.concatenate([vb, vb], axis=1), wide)
                values.append((out_k, c, part_k[:, c] + more))
                more = dot_nn(jnp.concatenate([kb, kb], axis=1), stack)
                values.append((out_v, c, part_v[:, c] + more))
        for ref, c, value in values:
            ref[:, c] = value.astype(jnp.bfloat16)

    def whole(buf, kind, j):
        return decode(jnp.concatenate([buf[kind, 2 * j], buf[kind, 2 * j + 1]], axis=0))

    def back_group(g):
        return [lax.rem(pair + g * GROUP + n, OWN) for n in range(GROUP)]

    def pass_on(kind):
        for g in range(OWN // GROUP):
            slots = 2 * GROUP - (1 if g == 0 else 0)
            drain(recv3.at[kind, pl.ds(0, slots)], s3_recv.at[kind, g])
            for j in back_group(g):
                forward(kind, j).start()

    def own_heads(kind):
        def step(g, _):
            slots = back_group(g)
            heads = [core * OWN + j for j in slots]
            finish(
                kind,
                heads,
                [
                    whole(recv3, kind, j) + level2(kind, h) * decode(from_core[kind, j])
                    for j, h in zip(slots, heads)
                ],
            )
            return 0

        lax.fori_loop(0, OWN // GROUP, step, 0)

    def other_heads(kind):
        for g in range(OWN // GROUP):
            slots = back_group(g)
            drain(fwd3.at[kind, pl.ds(0, 2 * GROUP)], f_recv.at[kind, g])
            heads = [(1 - core) * OWN + j for j in slots]
            finish(
                kind,
                heads,
                [
                    whole(fwd3, kind, j) + level2(kind, h) * decode(from_core_x[j])
                    for j, h in zip(slots, heads)
                ],
            )

    def drain_late():
        for g in range(OWN // GROUP):
            drain(fwd3.at[1, pl.ds(0, 2 * GROUP)], f_recv.at[1, g])
        for kind in range(2):
            drain(send3.at[kind, pl.ds(0, PLANE - 1)], s3_send.at[kind])
            drain(fwd3.at[kind], f_send.at[kind])

    def finish_all(kind):
        pass_on(kind)
        own_heads(kind)
        if kind == 0:
            other_heads(kind)

    in_order(finish_all)
    drain_late()


def store(
    out_q, out_k, out_v, fwd3, base_x, part_k, part_v, ks, vs, q_hbm, k_hbm, v_hbm,
    more_k, more_v, sem,
):
    core = lax.axis_index("head")
    width = OWN * DH
    own = pl.ds(pl.multiple_of(core * width, width), width)
    part = TOK // STORE_PARTS
    for p in range(STORE_PARTS):
        rows = pl.ds(p * part, part)
        pltpu.make_async_copy(out_k.at[rows, own], k_hbm.at[rows, own], sem.at[1]).start()
        pltpu.make_async_copy(out_v.at[rows, own], v_hbm.at[rows, own], sem.at[2]).start()
        pltpu.make_async_copy(out_q.at[rows], q_hbm.at[rows], sem.at[0]).start()
    for g in range(OWN // GROUP):
        values = []
        for j in range(g * GROUP, (g + 1) * GROUP):
            c = pl.ds(pl.multiple_of((1 - core) * width + j * DH, DH), DH)
            coded = jnp.concatenate([fwd3[1, 2 * j], fwd3[1, 2 * j + 1]], axis=0)
            hi, lo = split(decode(coded) + base_x[j])
            vb, kb = vs[:, c], ks[:, c]
            wide = jnp.concatenate([hi, lo], axis=1)
            stack = jnp.concatenate([hi, lo], axis=0)
            k_more = dot_nt(jnp.concatenate([vb, vb], axis=1), wide)
            v_more = dot_nn(jnp.concatenate([kb, kb], axis=1), stack)
            values.append((j, part_k[:, c] + k_more, part_v[:, c] + v_more))
        for j, k_new, v_new in values:
            more_k[:, j * DH : (j + 1) * DH] = k_new.astype(jnp.bfloat16)
            more_v[:, j * DH : (j + 1) * DH] = v_new.astype(jnp.bfloat16)
        size = GROUP * DH
        here = pl.ds(g * size, size)
        there = pl.ds(pl.multiple_of((1 - core) * width + g * size, size), size)
        for p in range(2):
            rows = pl.ds(p * BLOCK, BLOCK)
            pltpu.make_async_copy(more_k.at[rows, here], k_hbm.at[rows, there], sem.at[1]).start()
            pltpu.make_async_copy(more_v.at[rows, here], v_hbm.at[rows, there], sem.at[2]).start()
    for n, ref in enumerate((out_q, out_k, out_v)):
        pltpu.make_async_copy(ref, ref, sem.at[n]).wait()


def body(queries, key_rows, values, out_grad, level_weights):
    hbm = pl.BlockSpec(memory_space=pltpu.HBM)
    vmem = pl.BlockSpec(memory_space=pltpu.VMEM)
    bf, f32 = jnp.bfloat16, jnp.float32
    dma = pltpu.SemaphoreType.DMA
    rows = (TOK, HEADS * DH)
    out = jax.ShapeDtypeStruct(rows, bf)
    pinned = [
        pltpu.with_memory_space_constraint(a, pltpu.HBM)
        for a in (level_weights, queries, key_rows, values, out_grad)
    ]
    grads = pl.pallas_call(
        kernel,
        name="fenwick",
        out_shape=(pltpu.VMEM(rows, bf),) * 3
        + (
            pltpu.VMEM((2, PLANE, HALF, DH), bf),
            pltpu.VMEM((OWN, DH, DH), f32),
            pltpu.VMEM(rows, f32),
            pltpu.VMEM(rows, f32),
            pltpu.VMEM(rows, bf),
            pltpu.VMEM(rows, bf),
        ),
        in_specs=[hbm] * 5,
        out_specs=(vmem,) * 9,
        scratch_shapes=[pltpu.SMEM((HEADS, 11), f32)]
        + [pltpu.VMEM(rows, bf)] * 2
        + [
            pltpu.VMEM((2, OWN, DH, DH), f32),
            pltpu.VMEM((2, OWN, DH, DH), bf),
            pltpu.VMEM((OWN, DH, DH), bf),
            pltpu.VMEM((2, OWN, DH, DH), bf),
            pltpu.VMEM((OWN, DH, DH), bf),
            pltpu.VMEM((2, PLANE, HALF, DH), bf),
            pltpu.VMEM((2, PLANE, HALF, DH), bf),
            pltpu.VMEM((2, HALF, DH), bf),
            pltpu.VMEM((NZ - 1, HALF, DH), bf),
            pltpu.VMEM((HALF, DH), f32),
            pltpu.VMEM((2, PLANE, HALF, DH), bf),
            pltpu.VMEM((2, PLANE, HALF, DH), bf),
            pltpu.VMEM((2, PLANE, HALF, DH), f32),
        ]
        + [pltpu.VMEM(rows, f32)]
        + [
            dma((5,)),
            dma((2,)),
            dma((2, OWN // GROUP)),
            dma,
            dma,
            pltpu.SemaphoreType.REGULAR,
            dma((2,)),
            dma((2,)),
            dma,
            dma((NZ - 1,)),
            dma((2,)),
            dma((2, OWN // GROUP)),
            dma((2,)),
            dma((2, OWN // GROUP)),
        ],
        compiler_params=pltpu.CompilerParams(
            collective_id=0, has_side_effects=True, vmem_limit_bytes=40 << 20
        ),
    )(*pinned)
    return tuple(
        pl.pallas_call(
            store,
            name="store",
            out_shape=(out, out, out),
            in_specs=[vmem] * 9,
            out_specs=(hbm,) * 3,
            scratch_shapes=[pltpu.VMEM((TOK, OWN * DH), bf)] * 2 + [dma((3,))],
            compiler_params=pltpu.CompilerParams(vmem_limit_bytes=8 << 20),
        )(*(pltpu.with_memory_space_constraint(g, pltpu.VMEM) for g in grads))
    )


def solution(mesh):
    rows = P(("seq", "head"), None)
    return jax.shard_map(
        body,
        mesh=mesh,
        in_specs=(rows, rows, rows, rows, P()),
        out_specs=(rows, rows, rows),
        check_vma=False,
    )
```
